32 devices in a mesh: wide: 8 (over z, y), deep: 4 (over x, core).
Axes of the slice: x: 2, y: 2, z: 4, core: 2. Of those that a mesh axis runs over, the one named last changes fastest.
Arguments:
- coarse_density: float32 [64, 8, 480], P('wide', None, 'deep'), may hold values from 0.8 to 1.6
- coarse_velocity: float32 [3, 64, 8, 480], P(None, 'wide', None, 'deep'), may hold values from -0.4 to 0.4
- coarse_pressure: float32 [64, 8, 480], P('wide', None, 'deep'), may hold values from 0.8 to 1.6
- fine_density: float32 [4, 32, 16, 256], P('deep', 'wide'), may hold values from 0.8 to 1.6
- fine_velocity: float32 [4, 32, 3, 16, 256], P('deep', 'wide'), may hold values from -0.4 to 0.4
- fine_pressure: float32 [4, 32, 16, 256], P('deep', 'wide'), may hold values from 0.8 to 1.6
- patch_count: int32 [4, 8], P('deep'), may hold values from 1 to 4, 16 in all within a row
- region_start: int32 [4], P('deep'), may hold values from 0 to 103
Outputs:
- coarse_state: float32 [5, 64, 8, 480], P(None, 'wide', None, 'deep')
- fine_state: float32 [4, 32, 5, 16, 256], P('deep', 'wide')
The draws below stay inside these ranges and needn't reach their ends.
Inputs may be any that keep to these rules, and one draw needn't show every extreme that they name: `patch_count`: each deep row's counts sum to 16, and some device of every row holds 4 patches.
All inputs are finite; a program needn't handle non-finite values.
Results may differ from the reference program's by a relative error of at most 0.0003.
Values sent between devices are 32-bit elements; how exact they have to be, the bound alone decides.
A program may use at most 192 MiB of HBM per device.

```python
import math
import jax
import jax.numpy as jnp
import numpy as np
from jax import lax

PATCH = 16
SLOTS = 4
CZ = 120
BLOCK = 8
PLACES = 13
NX = 64
NY = 8
NZ = 480
NPATCH = 128
TOT_ROW = 16
N_WIDE = 8
N_DEEP = 4


def touch_ends(values, own_key, least, top_value):
    shape = values.shape
    index_at = [jax.random.randint(jax.random.fold_in(own_key, axis), (), 0, shape[axis]) for axis in range(len(shape))]
    values = values.at[tuple(index_at)].set(least)
    longest = shape.index(max(shape))
    index_at[longest] = (index_at[longest] + 1) % shape[longest]
    return values.at[tuple(index_at)].set(top_value)


def block_scale(stream_key, extent, cuts, smallest, top_value):
    gain, own = 1.0, jax.random.fold_in(stream_key, 6)
    for position, shards_of in cuts:
        heights = jnp.exp(jax.random.uniform(jax.random.fold_in(own, position), (shards_of,), jnp.float32, smallest / len(cuts), top_value / len(cuts)))
        gain = gain * jnp.repeat(heights, extent[position] // shards_of).reshape([-1 if axis == position else 1 for axis in range(len(extent))])
    return gain


def length_profile(amount, total, limit, skew):
    portions = [(1 << 20) // math.isqrt(standing ** skew) + 1 for standing in range(2, amount + 1)]
    rest, given = total - limit - (amount - 1), [1] * (amount - 1)
    while rest > 0:
        movable = [i for i in range(amount - 1) if given[i] < limit]
        pool, left = sum([portions[i] for i in movable]), rest
        for i in movable:
            extra = min(limit - given[i], max(1, left * portions[i] // pool), rest)
            given[i] = given[i] + extra
            rest = rest - extra
    return np.array([limit] + given)


def uneven(rng, count, total, reach, slope):
    if count == 2:
        one = jax.random.randint(rng, (), max(1, total - reach), min(reach, total - 1) + 1)
        return jnp.stack([one, total - one])
    tallies = jnp.asarray(length_profile(count, total, reach, slope), jnp.int32)
    twos = (count - 1) // 2
    source_of, receiver = tallies[1:1 + 2 * twos:2], tallies[2:2 + 2 * twos:2]
    margin = jnp.minimum(source_of - 1, reach - receiver)
    moved = jax.random.randint(jax.random.fold_in(rng, 1), (twos,), 0, 1 << 20) % (margin + 1)
    tallies = tallies.at[1:1 + 2 * twos:2].set(source_of - moved).at[2:2 + 2 * twos:2].set(receiver + moved)
    return tallies[jax.random.permutation(jax.random.fold_in(rng, 2), count)]


def setup_inputs(seed: int = 0) -> dict:
    splits = jax.random.split(jax.random.key(seed), 9)
    coarse_density = jnp.clip(jnp.exp(math.log(1.6) - 0.6931472 * jax.random.uniform(splits[0], (NX, NY, NZ), jnp.float32) ** block_scale(splits[0], (NX, NY, NZ), ((0, 8), (2, 4)), -0.2, 0.2)), 0.8, 1.6)
    coarse_velocity = jnp.clip(jax.random.uniform(splits[1], (3, NX, NY, NZ), jnp.float32, -0.4, 0.4) * block_scale(splits[1], (3, NX, NY, NZ), ((1, 8), (3, 4)), -0.4, 0.0), -0.4, 0.4)
    coarse_pressure = jnp.clip(jnp.exp(math.log(1.6) - 0.6931472 * jax.random.uniform(splits[2], (NX, NY, NZ), jnp.float32) ** block_scale(splits[2], (NX, NY, NZ), ((0, 8), (2, 4)), -0.2, 0.2)), 0.8, 1.6)
    fine_density = jnp.clip(jnp.exp(math.log(1.6) - 0.6931472 * jax.random.uniform(splits[3], (N_DEEP, N_WIDE * SLOTS, PATCH, PATCH * PATCH), jnp.float32) ** block_scale(splits[3], (N_DEEP, N_WIDE * SLOTS, PATCH, PATCH * PATCH), ((0, 4), (1, 8)), -0.2, 0.2)), 0.8, 1.6)
    fine_velocity = jnp.clip(jax.random.uniform(splits[4], (N_DEEP, N_WIDE * SLOTS, 3, PATCH, PATCH * PATCH), jnp.float32, -0.4, 0.4) * block_scale(splits[4], (N_DEEP, N_WIDE * SLOTS, 3, PATCH, PATCH * PATCH), ((0, 4), (1, 8)), -0.4, 0.0), -0.4, 0.4)
    fine_pressure = jnp.clip(jnp.exp(math.log(1.6) - 0.6931472 * jax.random.uniform(splits[5], (N_DEEP, N_WIDE * SLOTS, PATCH, PATCH * PATCH), jnp.float32) ** block_scale(splits[5], (N_DEEP, N_WIDE * SLOTS, PATCH, PATCH * PATCH), ((0, 4), (1, 8)), -0.2, 0.2)), 0.8, 1.6)
    patch_count = jax.vmap(lambda own: uneven(own, N_WIDE, TOT_ROW, SLOTS, 4))(jax.random.split(splits[6], N_DEEP)).reshape((N_DEEP, N_WIDE)).astype(jnp.int32)
    region_start = touch_ends(jax.random.randint(splits[7], (N_DEEP,), 0, N_WIDE * PLACES), jax.random.fold_in(splits[7], 1), 0, (N_WIDE * PLACES) - 1).astype(jnp.int32)
    return {"coarse_density": coarse_density, "coarse_velocity": coarse_velocity, "coarse_pressure": coarse_pressure, "fine_density": fine_density, "fine_velocity": fine_velocity, "fine_pressure": fine_pressure, "patch_count": patch_count, "region_start": region_start}


heat_ratio = 1.4
weno_floor = 1e-06
coarse_step = 0.2
fine_step = 0.1
fine_spacing = 0.5

def primitive(state):
    density = state[0]
    speed_x = state[1] / density
    speed_y = state[2] / density
    speed_z = state[3] / density
    kinetic = 0.5 * density * (speed_x * speed_x + speed_y * speed_y + speed_z * speed_z)
    pressure = (heat_ratio - 1.0) * (state[4] - kinetic)
    return jnp.stack([density, speed_x, speed_y, speed_z, pressure])

def conserved(prims):
    density = prims[0]
    kinetic = 0.5 * density * (prims[1] * prims[1] + prims[2] * prims[2] + prims[3] * prims[3])
    energy = prims[4] / (heat_ratio - 1.0) + kinetic
    return jnp.stack([density, density * prims[1], density * prims[2], density * prims[3], energy])

def weno_value(first, second, third, fourth, fifth):
    cand_one = (2.0 * first - 7.0 * second + 11.0 * third) / 6.0
    cand_two = (-second + 5.0 * third + 2.0 * fourth) / 6.0
    cand_three = (2.0 * third + 5.0 * fourth - fifth) / 6.0
    rough_one = 13.0 / 12.0 * (first - 2.0 * second + third) ** 2 + 0.25 * (first - 4.0 * second + 3.0 * third) ** 2
    rough_two = 13.0 / 12.0 * (second - 2.0 * third + fourth) ** 2 + 0.25 * (second - fourth) ** 2
    rough_three = 13.0 / 12.0 * (third - 2.0 * fourth + fifth) ** 2 + 0.25 * (3.0 * third - 4.0 * fourth + fifth) ** 2
    weight_one = 0.1 / (weno_floor + rough_one) ** 2
    weight_two = 0.6 / (weno_floor + rough_two) ** 2
    weight_three = 0.3 / (weno_floor + rough_three) ** 2
    total = weight_one + weight_two + weight_three
    return (weight_one * cand_one + weight_two * cand_two + weight_three * cand_three) / total

def wave_parts(dens, normal, side, other, press, wave, middle):
    energy = press / (heat_ratio - 1.0) + 0.5 * dens * (normal * normal + side * side + other * other)
    mass = dens * (wave - normal)
    state = jnp.stack([dens, dens * normal, dens * side, dens * other, energy])
    flux = jnp.stack([dens * normal, dens * normal * normal + press, dens * normal * side, dens * normal * other, normal * (energy + press)])
    factor = mass / (wave - middle)
    star = factor * jnp.stack([jnp.ones_like(dens), middle, side, other, energy / dens + (middle - normal) * (middle + press / mass)])
    return (flux, flux + wave * (star - state))

def hllc(left, right):
    sound_left = jnp.sqrt(heat_ratio * left[4] / left[0])
    sound_right = jnp.sqrt(heat_ratio * right[4] / right[0])
    slow = jnp.minimum(left[1] - sound_left, right[1] - sound_right)
    fast = jnp.maximum(left[1] + sound_left, right[1] + sound_right)
    mass_left = left[0] * (slow - left[1])
    mass_right = right[0] * (fast - right[1])
    middle = (right[4] - left[4] + mass_left * left[1] - mass_right * right[1]) / (mass_left - mass_right)
    flux_left, star_left = wave_parts(left[0], left[1], left[2], left[3], left[4], slow, middle)
    flux_right, star_right = wave_parts(right[0], right[1], right[2], right[3], right[4], fast, middle)
    return jnp.where(slow[None] >= 0.0, flux_left, jnp.where(middle[None] >= 0.0, star_left, jnp.where(fast[None] > 0.0, star_right, flux_right)))

def face_flux(padded, axis):
    prims = primitive(padded)
    count = padded.shape[axis] - 5
    pieces = [lax.slice_in_dim(prims, k, k + count, axis=axis) for k in range(6)]
    left = weno_value(pieces[0], pieces[1], pieces[2], pieces[3], pieces[4])
    right = weno_value(pieces[5], pieces[4], pieces[3], pieces[2], pieces[1])
    order = [0, axis] + [k for k in (1, 2, 3) if k != axis] + [4]
    inverse = [order.index(k) for k in range(5)]
    flux = hllc(left[np.array(order)], right[np.array(order)])
    return flux[np.array(inverse)]

def cell_rates(pad_x, pad_y, pad_z, spacing):
    flux_x = face_flux(pad_x, 1)
    flux_y = face_flux(pad_y, 2)
    flux_z = face_flux(pad_z, 3)
    change = flux_x[:, 1:] - flux_x[:, :-1] + (flux_y[:, :, 1:] - flux_y[:, :, :-1]) + (flux_z[:, :, :, 1:] - flux_z[:, :, :, :-1])
    return (-change / spacing, flux_x, flux_z)

def patch_rates(state, ghost_xl, ghost_xh, ghost_zl, ghost_zh):
    pad_x = jnp.concatenate([ghost_xl, state, ghost_xh], axis=1)
    pad_y = jnp.concatenate([state[:, :, -3:], state, state[:, :, :3]], axis=2)
    pad_z = jnp.concatenate([ghost_zl, state, ghost_zh], axis=3)
    rate, flux_x, flux_z = cell_rates(pad_x, pad_y, pad_z, fine_spacing)
    return (rate, flux_x[:, 0], flux_x[:, -1], flux_z[:, :, :, 0], flux_z[:, :, :, -1])

def coarse_ghosts(rim_x, rim_z):

    def spread(part, first_axis, second_axis):
        return jnp.repeat(jnp.repeat(part, 2, axis=first_axis), 2, axis=second_axis)
    low_x = spread(rim_x[:, np.array([0, 1, 1])], 2, 3)
    high_x = spread(rim_x[:, np.array([2, 2, 3])], 2, 3)
    low_z = spread(rim_z[..., np.array([0, 1, 1])], 1, 2)
    high_z = spread(rim_z[..., np.array([2, 2, 3])], 1, 2)
    return (low_x, high_x, low_z, high_z)

def coarsen(face):
    half = face.shape[-1] // 2
    return face.reshape(face.shape[:-2] + (half, 2, half, 2)).sum(axis=(-3, -1)) * 0.25

def average(state):
    half = state.shape[-1] // 2
    return state.reshape(state.shape[:-3] + (half, 2, half, 2, half, 2)).sum(axis=(-5, -3, -1)) * 0.125

def coarse_rates(state):
    padded_z = jnp.pad(state, ((0, 0), (0, 0), (0, 0), (3, 3)), mode='wrap')

    def one_row(row):
        slab = lax.dynamic_slice_in_dim(padded_z, row * CZ, CZ + 6, axis=3)
        centre = slab[:, :, :, 3:-3]
        pad_x = jnp.pad(centre, ((0, 0), (3, 3), (0, 0), (0, 0)), mode='wrap')
        pad_y = jnp.pad(centre, ((0, 0), (0, 0), (3, 3), (0, 0)), mode='wrap')
        return cell_rates(pad_x, pad_y, slab, 1.0)
    rate, flux_x, flux_z = lax.map(one_row, jnp.arange(N_DEEP, dtype=jnp.int32))
    rate = jnp.moveaxis(rate, 0, 3).reshape(5, NX, NY, NZ)
    return (rate, flux_x, flux_z)

def patch_rims(state, start_x, start_z):
    zero = jnp.zeros((), jnp.int32)
    size = state.shape[1]
    sides = [lax.dynamic_slice(state, (zero, ((start_x + shift) % size).astype(jnp.int32), zero, start_z.astype(jnp.int32)), (5, 1, BLOCK, BLOCK))[:, 0] for shift in (-2, -1, BLOCK, BLOCK + 1)]
    tops = [lax.dynamic_slice(state, (zero, start_x.astype(jnp.int32), zero, (start_z + shift).astype(jnp.int32)), (5, BLOCK, BLOCK, 1))[:, :, :, 0] for shift in (-2, -1, BLOCK, BLOCK + 1)]
    return (jnp.stack(sides, axis=1), jnp.stack(tops, axis=3))

def reference(coarse_density, coarse_velocity, coarse_pressure, fine_density, fine_velocity, fine_pressure, patch_count, region_start):
    coarse = conserved(jnp.stack([coarse_density, coarse_velocity[0], coarse_velocity[1], coarse_velocity[2], coarse_pressure]))
    rate_one, flux_xa, flux_za = coarse_rates(coarse)
    middle = coarse + coarse_step * rate_one
    rate_two, flux_xb, flux_zb = coarse_rates(middle)
    updated = 0.5 * (coarse + middle + coarse_step * rate_two)
    mean_x = 0.5 * (flux_xa + flux_xb)
    mean_z = 0.5 * (flux_za + flux_zb)
    density = jnp.swapaxes(fine_density.reshape(NPATCH, PATCH, PATCH, PATCH), 2, 3)
    velocity = jnp.swapaxes(fine_velocity.reshape(NPATCH, 3, PATCH, PATCH, PATCH), 3, 4)
    pressure = jnp.swapaxes(fine_pressure.reshape(NPATCH, PATCH, PATCH, PATCH), 2, 3)
    initial = jnp.moveaxis(conserved(jnp.stack([density, velocity[:, 0], velocity[:, 1], velocity[:, 2], pressure])), 0, 1)
    index = jnp.arange(NPATCH, dtype=jnp.int32)
    rows = index // (N_WIDE * SLOTS)
    owners = index // SLOTS % N_WIDE
    places = index % SLOTS
    ends = jnp.cumsum(patch_count, axis=1).astype(jnp.int32)
    begins = ends - patch_count
    totals = ends[:, -1]
    blocks_all = N_WIDE * PLACES
    anchor = region_start[rows]
    alive = places < patch_count[rows, owners]
    serial = begins[rows, owners] + places
    ident = (anchor + 3 * (serial // 2) + serial % 2) % blocks_all
    column = ident % N_WIDE
    height = ident // N_WIDE

    def locate(target):
        offset = (target - anchor) % blocks_all
        part = offset % 3
        rank = 2 * (offset // 3) + part
        live = (part < 2) & (rank < totals[rows])
        owner = jnp.minimum(lax.optimization_barrier(jnp.sum((rank[:, None] >= ends[rows]).astype(jnp.int32), axis=1)), N_WIDE - 1)
        place = jnp.clip(rank - begins[rows, owner], 0, SLOTS - 1)
        return (live, (rows * N_WIDE + owner) * SLOTS + place)
    live_xl, flat_xl = locate(height * N_WIDE + (column + N_WIDE - 1) % N_WIDE)
    live_xh, flat_xh = locate(height * N_WIDE + (column + 1) % N_WIDE)
    live_zl, flat_zl = locate(ident - N_WIDE)
    live_zl = live_zl & (height > 0)
    live_zh, flat_zh = locate(ident + N_WIDE)
    live_zh = live_zh & (height < PLACES - 1)
    start_x = (column * BLOCK).astype(jnp.int32)
    start_z = (rows * CZ + (height + 1) * BLOCK).astype(jnp.int32)
    old_x, old_z = jax.vmap(patch_rims, (None, 0, 0))(coarse, start_x, start_z)
    new_x, new_z = jax.vmap(patch_rims, (None, 0, 0))(updated, start_x, start_z)

    def mark(flag):
        return flag[:, None, None, None, None]

    def fine_rates(states, theta):
        rim_x = (1.0 - theta) * old_x + theta * new_x
        rim_z = (1.0 - theta) * old_z + theta * new_z
        cxl, cxh, czl, czh = jax.vmap(coarse_ghosts)(rim_x, rim_z)
        ghost_xl = jnp.where(mark(live_xl), states[:, :, -3:][flat_xl], cxl)
        ghost_xh = jnp.where(mark(live_xh), states[:, :, :3][flat_xh], cxh)
        ghost_zl = jnp.where(mark(live_zl), states[..., -3:][flat_zl], czl)
        ghost_zh = jnp.where(mark(live_zh), states[..., :3][flat_zh], czh)

        def one_patch(group):
            return patch_rates(group[0], group[1], group[2], group[3], group[4])
        return lax.map(one_patch, (states, ghost_xl, ghost_xh, ghost_zl, ghost_zh))

    def substep(states, theta_a, theta_b):
        early = fine_rates(states, theta_a)
        middle_f = states + fine_step * early[0]
        later = fine_rates(middle_f, theta_b)
        after = 0.5 * (states + middle_f + fine_step * later[0])
        faces = [fine_step * 0.5 * (a + b) for a, b in zip(early[1:], later[1:])]
        return (after, faces)
    halfway, faces_one = substep(initial, 0.0, 0.5)
    final_fine, faces_two = substep(halfway, 0.5, 1.0)
    registers = [coarsen(a + b) for a, b in zip(faces_one, faces_two)]
    averaged = average(final_fine)
    mask_xl = alive & ~live_xl
    mask_xh = alive & ~live_xh
    mask_zl = alive & ~live_zl
    mask_zh = alive & ~live_zh
    zero = jnp.zeros((), jnp.int32)

    def bump(field, piece, corner_x, corner_z):
        corner = (zero, corner_x.astype(jnp.int32), zero, corner_z.astype(jnp.int32))
        current = lax.dynamic_slice(field, corner, piece.shape)
        return lax.dynamic_update_slice(field, current + piece, corner)

    def add_one(patch, field):
        row = rows[patch]
        x_low = start_x[patch]
        local = ((height[patch] + 1) * BLOCK).astype(jnp.int32)
        z_low = start_z[patch]
        faces_x = lax.dynamic_index_in_dim(mean_x, row, 0, keepdims=False)
        faces_z = lax.dynamic_index_in_dim(mean_z, row, 0, keepdims=False)
        low = lax.dynamic_slice(faces_x, (zero, x_low, zero, local), (5, 1, BLOCK, BLOCK))
        delta = coarse_step * low - registers[0][patch][:, None]
        field = bump(field, jnp.where(mask_xl[patch], delta, 0.0), (x_low - 1) % NX, z_low)
        high = lax.dynamic_slice(faces_x, (zero, x_low + BLOCK, zero, local), (5, 1, BLOCK, BLOCK))
        delta = coarse_step * high - registers[1][patch][:, None]
        field = bump(field, jnp.where(mask_xh[patch], -delta, 0.0), (x_low + BLOCK) % NX, z_low)
        low = lax.dynamic_slice(faces_z, (zero, x_low, zero, local), (5, BLOCK, BLOCK, 1))
        delta = coarse_step * low - registers[2][patch][..., None]
        field = bump(field, jnp.where(mask_zl[patch], delta, 0.0), x_low, z_low - 1)
        high = lax.dynamic_slice(faces_z, (zero, x_low, zero, local + BLOCK), (5, BLOCK, BLOCK, 1))
        delta = coarse_step * high - registers[3][patch][..., None]
        field = bump(field, jnp.where(mask_zh[patch], -delta, 0.0), x_low, z_low + BLOCK)
        return field
    correction = lax.fori_loop(0, NPATCH, add_one, jnp.zeros_like(updated))
    combined = updated + correction

    def place_one(patch, field):
        corner = (zero, start_x[patch], zero, start_z[patch])
        current = lax.dynamic_slice(field, corner, (5, BLOCK, BLOCK, BLOCK))
        return lax.dynamic_update_slice(field, jnp.where(alive[patch], averaged[patch], current), corner)
    coarse_state = lax.fori_loop(0, NPATCH, place_one, combined)
    fine_final = jnp.where(mark(alive), final_fine, initial)
    fine_state = jnp.swapaxes(fine_final, 3, 4).reshape(N_DEEP, N_WIDE * SLOTS, 5, PATCH, PATCH * PATCH)
    return (coarse_state, fine_state)
```

```python
from functools import partial

import jax
import jax.numpy as jnp
import numpy as np
from jax import lax
from jax.experimental import pallas as pl
from jax.experimental.pallas import tpu as pltpu
from jax.sharding import PartitionSpec as P

heat_ratio = 1.4
weno_floor = 1e-06
coarse_step = 0.2
fine_step = 0.1
fine_spacing = 0.5
INTERPRET = False
HIGHEST = lax.Precision.HIGHEST


def primitive(state):
    density = state[0]
    speed_x = state[1] / density
    speed_y = state[2] / density
    speed_z = state[3] / density
    kinetic = 0.5 * density * (speed_x * speed_x + speed_y * speed_y + speed_z * speed_z)
    pressure = (heat_ratio - 1.0) * (state[4] - kinetic)
    return [density, speed_x, speed_y, speed_z, pressure]


def conserved(prims):
    density = prims[0]
    kinetic = 0.5 * density * (prims[1] * prims[1] + prims[2] * prims[2] + prims[3] * prims[3])
    energy = prims[4] / (heat_ratio - 1.0) + kinetic
    return jnp.stack([density, density * prims[1], density * prims[2], density * prims[3], energy])


def edge_values(v, e1, e2, e3, e4):
    s1, s2, s3 = e2 - e1, e3 - e2, e4 - e3
    t1, t2, t3 = 3.0 * e2 - e1, e2 + e3, 3.0 * e3 - e4
    b1 = weno_floor + (13.0 / 12.0) * (s1 * s1) + 0.25 * (t1 * t1)
    b2 = weno_floor + (13.0 / 12.0) * (s2 * s2) + 0.25 * (t2 * t2)
    b3 = weno_floor + (13.0 / 12.0) * (s3 * s3) + 0.25 * (t3 * t3)
    q1, q2, q3 = b1 * b1, b2 * b2, b3 * b3
    a = q2 * q3
    b = 6.0 * (q1 * q3)
    c = q1 * q2
    a3, c3 = 3.0 * a, 3.0 * c
    upper = v + (a * (5.0 * e2 - 2.0 * e1) + b * (e2 + 2.0 * e3) + c3 * (4.0 * e3 - e4)) / (
        6.0 * (a + b + c3)
    )
    lower = v - (c * (5.0 * e3 - 2.0 * e4) + b * (e3 + 2.0 * e2) + a3 * (4.0 * e2 - e1)) / (
        6.0 * (c + b + a3)
    )
    return upper, lower


def hllc(left, right, normal):
    rl, ul, pl_ = left[0], left[normal], left[4]
    rr, ur, pr = right[0], right[normal], right[4]
    sound_left = jnp.sqrt(heat_ratio * pl_ / rl)
    sound_right = jnp.sqrt(heat_ratio * pr / rr)
    slow = jnp.minimum(ul - sound_left, ur - sound_right)
    fast = jnp.maximum(ul + sound_left, ur + sound_right)
    mass_left = rl * (slow - ul)
    mass_right = rr * (fast - ur)
    middle = (pr - pl_ + mass_left * ul - mass_right * ur) / (mass_left - mass_right)
    use_left = (slow >= 0.0) | (middle >= 0.0)
    dens = jnp.where(use_left, rl, rr)
    vel = [None] + [jnp.where(use_left, left[k], right[k]) for k in (1, 2, 3)]
    press = jnp.where(use_left, pl_, pr)
    mass = jnp.where(use_left, mass_left, mass_right)
    wave = jnp.where(use_left, slow, fast)
    in_star = (use_left & (slow < 0.0)) | (jnp.logical_not(use_left) & (fast > 0.0))
    u = vel[normal]
    energy = press / (heat_ratio - 1.0) + 0.5 * dens * (
        vel[1] * vel[1] + vel[2] * vel[2] + vel[3] * vel[3]
    )
    flow = dens * u
    factor = mass / (wave - middle)
    star_energy = factor * (energy / dens + (middle - u) * (middle + press / mass))
    flux = [flow + jnp.where(in_star, wave * (factor - dens), 0.0)]
    for k in (1, 2, 3):
        base = flow * vel[k] + press if k == normal else flow * vel[k]
        star = factor * (middle if k == normal else vel[k])
        flux.append(base + jnp.where(in_star, wave * (star - dens * vel[k]), 0.0))
    flux.append(u * (energy + press) + jnp.where(in_star, wave * (star_energy - energy), 0.0))
    return flux


def shifted_flux(prims, normal, shift):
    left, right = [], []
    for v in prims:
        d = shift(v, 1) - v
        upper, lower = edge_values(v, shift(d, -2), shift(d, -1), d, shift(d, 1))
        left.append(upper)
        right.append(shift(lower, 1))
    return hllc(left, right, normal)


def roll(v, step, axis):
    return pltpu.roll(v, step % v.shape[axis], axis)


def fine_kernel(second, edge, base_ref, cur_ref, pad_x_ref, pad_z_ref, out_ref, fx_ref, fz_ref):
    cells = edge * edge
    prims = primitive([pad_x_ref[0, k] for k in range(5)])
    flux = shifted_flux(prims, 1, lambda v, k: roll(v, -k, 0))
    for k in range(5):
        fx_ref[0, k] = flux[k]
        diff = flux[k] - roll(flux[k], 1, 0)
        out_ref[0, k] = roll(diff, -3, 0)[:edge]
    prims = primitive([cur_ref[0, k] for k in range(5)])
    ypos = lax.broadcasted_iota(jnp.int32, (edge, cells), 1) % edge

    def shift_y(v, k):
        step = k % edge
        return jnp.where(ypos < edge - step, roll(v, -step, 1), roll(v, edge - step, 1))

    flux = shifted_flux(prims, 2, shift_y)
    for k in range(5):
        out_ref[0, k] += flux[k] - shift_y(flux[k], -1)
    prims = primitive([pad_z_ref[0, k] for k in range(5)])
    flux = shifted_flux(prims, 3, lambda v, k: roll(v, -k * edge, 1))
    for k in range(5):
        fz_ref[0, k] = flux[k]
        diff = flux[k] - roll(flux[k], edge, 1)
        change = out_ref[0, k] + roll(diff, -3 * edge, 1)[:, :cells]
        new = cur_ref[0, k] - (fine_step / fine_spacing) * change
        out_ref[0, k] = 0.5 * (base_ref[0, k] + new) if second else new


def fine_stage(second, base, cur, pad_x, pad_z):
    count, _, edge, cells = cur.shape
    specs = [
        pl.BlockSpec((1,) + a.shape[1:], lambda i: (i, 0, 0, 0)) for a in (base, cur, pad_x, pad_z)
    ]
    return pl.pallas_call(
        partial(fine_kernel, second, edge),
        grid=(count,),
        in_specs=specs,
        out_specs=[specs[1], specs[2], specs[3]],
        out_shape=[jax.ShapeDtypeStruct(a.shape, jnp.float32) for a in (cur, pad_x, pad_z)],
        interpret=INTERPRET,
    )(base, cur, pad_x, pad_z)


def coarse_kernel(second, base_ref, cur_ref, ghost_ref, out_ref, fx_ref, fz_ref):
    block = cur_ref.shape[1]
    left, right = [], []
    whole = [
        jnp.concatenate([ghost_ref[k, :3], cur_ref[k], ghost_ref[k, 3:]], axis=0) for k in range(5)
    ]
    for v in primitive(whole):
        d = v[1:] - v[:-1]
        n = block + 2
        upper, lower = edge_values(v[2 : 2 + n], d[:n], d[1 : 1 + n], d[2 : 2 + n], d[3 : 3 + n])
        left.append(upper[:-1])
        right.append(lower[1:])
    flux = hllc(left, right, 1)
    for k in range(5):
        fx_ref[k, 0] = flux[k][0]
        fx_ref[k, 1] = flux[k][block]
        out_ref[k] = flux[k][1:] - flux[k][:-1]
    prims = primitive([cur_ref[k] for k in range(5)])
    flux = shifted_flux(prims, 2, lambda v, k: roll(v, -k, 1))
    for k in range(5):
        out_ref[k] += flux[k] - roll(flux[k], 1, 1)
    prims = primitive([cur_ref[k] for k in range(5)])
    flux = shifted_flux(prims, 3, lambda v, k: roll(v, -k, 2))
    for k in range(5):
        fz_ref[k] = flux[k]
        change = out_ref[k] + flux[k] - roll(flux[k], 1, 2)
        new = cur_ref[k] - coarse_step * change
        out_ref[k] = 0.5 * (base_ref[k] + new) if second else new


def coarse_stage(second, base, state, layers, below, above):
    depth = state.shape[3]
    lanes = -(-(depth + 6) // 128) * 128
    cur = jnp.concatenate([below, state, above, state[..., : lanes - depth - 6]], axis=3)
    wide = [(0, 0, 0)] * 3 + [(3, lanes - depth - 3, 0)]
    one = jnp.float32(1.0)
    ghost = lax.pad(layers, one, wide)
    base = lax.pad(base, one, wide)
    shapes = [cur.shape, (5, 2) + cur.shape[2:], cur.shape]
    out, fx, fz = pl.pallas_call(
        partial(coarse_kernel, second),
        out_shape=[jax.ShapeDtypeStruct(s, jnp.float32) for s in shapes],
        interpret=INTERPRET,
    )(base, cur, ghost)
    return out[..., 3 : 3 + depth], fx[..., 3 : 3 + depth], fz[..., 2 : 3 + depth]


def ring(count):
    up = [(i, (i + 1) % count) for i in range(count)]
    return up, [(j, i) for i, j in up]


def halo(shard, axis, dim, width):
    up, down = ring(lax.axis_size(axis))
    length = shard.shape[dim]
    before = lax.ppermute(lax.slice_in_dim(shard, length - width, length, axis=dim), axis, up)
    after = lax.ppermute(lax.slice_in_dim(shard, 0, width, axis=dim), axis, down)
    return before, after


def mark(flag):
    return flag[:, None, None, None]


def select(flags, values):
    which = jnp.sum(
        flags.astype(jnp.int32) * jnp.arange(flags.shape[1], dtype=jnp.int32)[None], axis=1
    )
    return values[which]


def exchange(values):
    return lax.all_to_all(values, "wide", split_axis=0, concat_axis=0, tiled=True)


def spread_matrices(block):
    edge = 2 * block
    fine = np.arange(edge)
    face = np.zeros((block, block, edge, edge), np.float32)
    face[fine[None] // 2, fine[:, None] // 2, fine[:, None], fine[None]] = 1.0
    face = face.reshape(block * block, edge * edge)
    top = np.zeros((block, 4, 2, 3, edge), np.float32)
    for side, chosen in enumerate(([0, 1, 1], [2, 2, 3])):
        for layer, source in enumerate(chosen):
            top[fine // 2, source, side, layer, fine] = 1.0
    return face, top.reshape(4 * block, 6 * edge)


def local(
    coarse_density,
    coarse_velocity,
    coarse_pressure,
    fine_density,
    fine_velocity,
    fine_pressure,
    patch_count,
    region_start,
):
    width = lax.axis_size("wide")
    here = lax.axis_index("wide")
    block = coarse_density.shape[0]
    depth = coarse_density.shape[2]
    places = depth // block - 2
    slots = fine_density.shape[1]
    edge = 2 * block
    cells = edge * edge
    blocks_all = width * places
    counts = patch_count[0]
    ends = jnp.cumsum(counts)
    begins = ends - counts
    total = ends[-1]
    anchor = region_start[0]
    face_matrix, top_matrix = spread_matrices(block)

    def locate(target):
        offset = (target - anchor) % blocks_all
        part = offset % 3
        rank = 2 * (offset // 3) + part
        live = (part < 2) & (rank < total)
        return live, jnp.minimum(offset // 3, width - 1)

    dest = jnp.arange(width, dtype=jnp.int32)
    pair = jnp.arange(2, dtype=jnp.int32)

    density = fine_density[0]
    velocity = fine_velocity[0]
    pressure = fine_pressure[0]
    initial = jnp.moveaxis(
        conserved(jnp.stack([density, velocity[:, 0], velocity[:, 1], velocity[:, 2], pressure])),
        0,
        1,
    )
    wanted = jnp.clip(2 * dest[:, None] + pair[None] - begins[here], 0, slots - 1)
    moved = exchange(initial[wanted])
    my_rank = 2 * here + pair
    holder = jnp.minimum(
        jnp.sum((my_rank[:, None] >= ends[None]).astype(jnp.int32), axis=1), width - 1
    )
    start = jnp.stack([moved[holder[0], 0], moved[holder[1], 1]])

    coarse = conserved(
        jnp.stack(
            [
                coarse_density,
                coarse_velocity[0],
                coarse_velocity[1],
                coarse_velocity[2],
                coarse_pressure,
            ]
        )
    )
    old_xl, old_xh = halo(coarse, "wide", 1, 3)
    zl, zh = halo(coarse, "deep", 3, 3)
    middle, early_x, early_z = coarse_stage(
        False, coarse, coarse, jnp.concatenate([old_xl, old_xh], axis=1), zl, zh
    )
    xl, xh = halo(middle, "wide", 1, 3)
    zl, zh = halo(middle, "deep", 3, 3)
    updated, later_x, later_z = coarse_stage(
        True, coarse, middle, jnp.concatenate([xl, xh], axis=1), zl, zh
    )
    mean_x = 0.5 * (early_x + later_x)
    mean_z = 0.5 * (early_z + later_z)
    new_xl, new_xh = halo(updated, "wide", 1, 2)

    def side_items(low, high):
        side = jnp.concatenate([low[:, -2:], high[:, :2]], axis=1)
        cut = side[..., block : block * (places + 1)].reshape(5, 4, block, places, block)
        return jnp.moveaxis(cut, 3, 0).reshape(places, -1)

    def top_items(state):
        blocked = state.reshape(5, block, block, places + 2, block)
        cut = jnp.concatenate([blocked[..., :-2, -2:], blocked[..., 2:, :2]], axis=-1)
        return jnp.moveaxis(cut, 3, 0).reshape(places, -1)

    items = jnp.concatenate(
        [side_items(old_xl, old_xh), side_items(new_xl, new_xh), top_items(coarse), top_items(updated)],
        axis=1,
    ).reshape(places, -1, 128)
    height_ids = jnp.arange(places, dtype=jnp.int32)
    local_ident = height_ids * width + here
    live_here, device_here = locate(local_ident)
    to_device = live_here[None] & (device_here[None] == dest[:, None])
    received = exchange(select(to_device, items))

    my_ident = (anchor + 3 * here + pair) % blocks_all
    my_column = my_ident % width
    my_height = my_ident // width
    rims = received[my_column].reshape(2, 4, 5, -1)
    side_rims = rims[:, :2].reshape(2, 2, 5, 4, block * block)
    side_ghosts = jnp.dot(side_rims, face_matrix, precision=HIGHEST)
    side_ghosts = jnp.concatenate(
        [
            side_ghosts[:, :, :, 0:2],
            side_ghosts[:, :, :, 1:3],
            side_ghosts[:, :, :, 2:4],
        ],
        axis=3,
    )
    top_rims = rims[:, 2:].reshape(2, 2, 5, block, 4 * block)
    top_ghosts = jnp.repeat(jnp.dot(top_rims, top_matrix, precision=HIGHEST), 2, axis=3)

    wrap_low = my_column == 0
    wrap_high = my_column == width - 1
    row_ident = my_height * width
    live_xl = locate(row_ident + (my_column + width - 1) % width)[0]
    live_xh = locate(row_ident + (my_column + 1) % width)[0]
    live_zl = locate(my_ident - width)[0] & (my_height > 0)
    live_zh = locate(my_ident + width)[0] & (my_height < places - 1)

    def partner(slabs, distance):
        found = []
        for slot in range(2):
            shift, other = divmod(slot + distance, 3)
            if other == 2:
                found.append(jnp.zeros_like(slabs[0]))
            elif shift == 0:
                found.append(slabs[other])
            else:
                perm = [(i + shift, i) for i in range(width) if 0 <= i + shift < width]
                found.append(lax.ppermute(slabs[other], "wide", perm))
        return jnp.stack(found)

    def fine_pads(states, theta):
        low_x, high_x = states[:, :, :3], states[:, :, -3:]
        low_z, high_z = states[..., : 3 * edge], states[..., -3 * edge :]
        from_xl = jnp.where(mark(wrap_low), partner(high_x, width - 1), partner(high_x, -1))
        from_xh = jnp.where(mark(wrap_high), partner(low_x, 1 - width), partner(low_x, 1))
        from_zl = partner(high_z, -width)
        from_zh = partner(low_z, width)
        side = (1.0 - theta) * side_ghosts[:, 0] + theta * side_ghosts[:, 1]
        top = (1.0 - theta) * top_ghosts[:, 0] + theta * top_ghosts[:, 1]
        xl = jnp.where(mark(live_xl), from_xl, side[:, :, 0:3])
        xh = jnp.where(mark(live_xh), from_xh, side[:, :, 3:6])
        zl = jnp.where(mark(live_zl), from_zl, top[..., : 3 * edge])
        zh = jnp.where(mark(live_zh), from_zh, top[..., 3 * edge :])
        rows = -(-(edge + 6) // 8) * 8
        lanes = -(-(cells + 6 * edge) // 128) * 128
        pad_x = jnp.concatenate([xl, states, xh, states[:, :, : rows - edge - 6]], axis=2)
        pad_z = jnp.concatenate([zl, states, zh, states[..., : lanes - cells - 6 * edge]], axis=3)
        return pad_x, pad_z

    states = start
    faces = []
    for theta_a, theta_b in ((0.0, 0.5), (0.5, 1.0)):
        first, fx, fz = fine_stage(False, states, states, *fine_pads(states, theta_a))
        faces.append((fx, fz))
        states, fx, fz = fine_stage(True, states, first, *fine_pads(first, theta_b))
        faces.append((fx, fz))

    back = exchange(jnp.broadcast_to(states[None], (width,) + states.shape))
    slot_ids = jnp.arange(slots, dtype=jnp.int32)
    my_alive = slot_ids < counts[here]
    serial = jnp.clip(begins[here] + slot_ids, 0, 2 * width - 1)
    final_fine = back.reshape((2 * width,) + back.shape[2:])[serial]
    fine_out = jnp.where(mark(my_alive), final_fine, initial)[None]

    face_mean = face_matrix.T * 0.25
    low_face = sum(fx[:, :, 2] for fx, _ in faces)
    high_face = sum(fx[:, :, edge + 2] for fx, _ in faces)
    side_regs = jnp.dot(
        jnp.stack([low_face, high_face], axis=1), face_mean * (0.5 * fine_step), precision=HIGHEST
    )
    bottom = sum(fz[..., 2 * edge : 3 * edge] for _, fz in faces)
    ceiling = sum(fz[..., 2 * edge + cells : 3 * edge + cells] for _, fz in faces)
    tops = jnp.stack([bottom, ceiling], axis=1).reshape(2, 2, 5, block, 2, edge).sum(axis=4)
    half = np.repeat(np.eye(block, dtype=np.float32), 2, axis=0) * (0.25 * 0.5 * fine_step)
    top_regs = jnp.dot(tops, half, precision=HIGHEST)
    pooled = states.reshape(2, 5, block, 2, cells).sum(axis=3)
    averaged = jnp.dot(pooled, face_mean * 0.5, precision=HIGHEST)
    package = jnp.concatenate(
        [averaged.reshape(2, -1), side_regs.reshape(2, -1), top_regs.reshape(2, -1)], axis=1
    ).reshape(2, -1, 128)
    to_brick = my_column[None] == dest[:, None]
    brought = exchange(select(to_brick, package))
    picked = brought[device_here].reshape(places, -1)
    cube = 5 * block * block * block
    avg_here = picked[:, :cube].reshape(places, 5, block, block, block)
    regs_here = picked[:, cube:].reshape(places, 4, 5, block, block)
    edge_xl = live_here & ~locate(height_ids * width + (here + width - 1) % width)[0]
    edge_xh = live_here & ~locate(height_ids * width + (here + 1) % width)[0]
    edge_zl = live_here & ~(locate(local_ident - width)[0] & (height_ids > 0))
    edge_zh = live_here & ~(locate(local_ident + width)[0] & (height_ids < places - 1))
    span = slice(block, block * (places + 1))

    def along_z(term):
        return jnp.moveaxis(term, 0, 2).reshape(5, block, places * block)

    low_mid = jnp.where(
        jnp.repeat(edge_xl, block),
        coarse_step * mean_x[:, 0, :, span] - along_z(regs_here[:, 0]),
        0.0,
    )
    high_mid = jnp.where(
        jnp.repeat(edge_xh, block),
        -(coarse_step * mean_x[:, 1, :, span] - along_z(regs_here[:, 1])),
        0.0,
    )
    up, down = ring(width)
    to_first = lax.ppermute(high_mid, "wide", up)
    to_last = lax.ppermute(low_mid, "wide", down)
    under = mean_z[..., :depth].reshape(5, block, block, places + 2, block)[..., 0]
    low_terms = coarse_step * under[..., 1:-1] - jnp.moveaxis(regs_here[:, 2], 0, 3)
    high_terms = coarse_step * under[..., 2:] - jnp.moveaxis(regs_here[:, 3], 0, 3)
    low_terms = jnp.where(edge_zl, low_terms, 0.0)
    high_terms = jnp.where(edge_zh, -high_terms, 0.0)
    none = ((0, 0),) * 3
    last_cell = jnp.pad(low_terms, none + ((0, 2),))[..., None]
    first_cell = jnp.pad(high_terms, none + ((2, 0),))[..., None]
    in_block = jnp.arange(block)
    correction = jnp.where(in_block == block - 1, last_cell, 0.0) + jnp.where(
        in_block == 0, first_cell, 0.0
    )
    result = updated + correction.reshape(updated.shape)
    ends_z = ((0, 0), (0, 0), (block, block))
    layer = jnp.arange(block)[None, :, None, None]
    result = result + jnp.where(layer == 0, jnp.pad(to_first, ends_z)[:, None], 0.0)
    result = result + jnp.where(layer == block - 1, jnp.pad(to_last, ends_z)[:, None], 0.0)
    avg_z = jnp.moveaxis(avg_here, 0, 3).reshape(5, block, block, places * block)
    avg_z = jnp.pad(avg_z, none + ((block, block),))
    covered = jnp.pad(jnp.repeat(live_here, block), (block, block))
    return jnp.where(covered, avg_z, result), fine_out


def solution(mesh):
    return jax.shard_map(
        local,
        mesh=mesh,
        in_specs=(
            P("wide", None, "deep"),
            P(None, "wide", None, "deep"),
            P("wide", None, "deep"),
            P("deep", "wide", None, None),
            P("deep", "wide", None, None, None),
            P("deep", "wide", None, None),
            P("deep", None),
            P("deep"),
        ),
        out_specs=(P(None, "wide", None, "deep"), P("deep", "wide", None, None, None)),
        check_vma=False,
    )
```

```python
from functools import partial

import jax
import jax.numpy as jnp
import numpy as np
from jax import lax
from jax.experimental import pallas as pl
from jax.experimental.pallas import tpu as pltpu
from jax.sharding import PartitionSpec as P

heat_ratio = 1.4
weno_floor = 1e-06
coarse_step = 0.2
fine_step = 0.1
fine_spacing = 0.5
INTERPRET = False
HIGHEST = lax.Precision.HIGHEST


def primitive(state):
    density = state[0]
    speed_x = state[1] / density
    speed_y = state[2] / density
    speed_z = state[3] / density
    kinetic = 0.5 * density * (speed_x * speed_x + speed_y * speed_y + speed_z * speed_z)
    pressure = (heat_ratio - 1.0) * (state[4] - kinetic)
    return [density, speed_x, speed_y, speed_z, pressure]


def conserved(prims):
    density = prims[0]
    kinetic = 0.5 * density * (prims[1] * prims[1] + prims[2] * prims[2] + prims[3] * prims[3])
    energy = prims[4] / (heat_ratio - 1.0) + kinetic
    return jnp.stack([density, density * prims[1], density * prims[2], density * prims[3], energy])


def edge_values(v, e1, e2, e3, e4):
    s1, s2, s3 = e2 - e1, e3 - e2, e4 - e3
    t1, t2, t3 = 3.0 * e2 - e1, e2 + e3, 3.0 * e3 - e4
    b1 = weno_floor + (13.0 / 12.0) * (s1 * s1) + 0.25 * (t1 * t1)
    b2 = weno_floor + (13.0 / 12.0) * (s2 * s2) + 0.25 * (t2 * t2)
    b3 = weno_floor + (13.0 / 12.0) * (s3 * s3) + 0.25 * (t3 * t3)
    q1, q2, q3 = b1 * b1, b2 * b2, b3 * b3
    a = q2 * q3
    b = 6.0 * (q1 * q3)
    c = q1 * q2
    a3, c3 = 3.0 * a, 3.0 * c
    upper = v + (a * (5.0 * e2 - 2.0 * e1) + b * (e2 + 2.0 * e3) + c3 * (4.0 * e3 - e4)) / (
        6.0 * (a + b + c3)
    )
    lower = v - (c * (5.0 * e3 - 2.0 * e4) + b * (e3 + 2.0 * e2) + a3 * (4.0 * e2 - e1)) / (
        6.0 * (c + b + a3)
    )
    return upper, lower


def hllc(left, right, normal):
    rl, ul, pl_ = left[0], left[normal], left[4]
    rr, ur, pr = right[0], right[normal], right[4]
    sound_left = jnp.sqrt(heat_ratio * pl_ / rl)
    sound_right = jnp.sqrt(heat_ratio * pr / rr)
    slow = jnp.minimum(ul - sound_left, ur - sound_right)
    fast = jnp.maximum(ul + sound_left, ur + sound_right)
    mass_left = rl * (slow - ul)
    mass_right = rr * (fast - ur)
    middle = (pr - pl_ + mass_left * ul - mass_right * ur) / (mass_left - mass_right)
    use_left = (slow >= 0.0) | (middle >= 0.0)
    dens = jnp.where(use_left, rl, rr)
    vel = [None] + [jnp.where(use_left, left[k], right[k]) for k in (1, 2, 3)]
    press = jnp.where(use_left, pl_, pr)
    mass = jnp.where(use_left, mass_left, mass_right)
    wave = jnp.where(use_left, slow, fast)
    in_star = (use_left & (slow < 0.0)) | (jnp.logical_not(use_left) & (fast > 0.0))
    u = vel[normal]
    energy = press / (heat_ratio - 1.0) + 0.5 * dens * (
        vel[1] * vel[1] + vel[2] * vel[2] + vel[3] * vel[3]
    )
    flow = dens * u
    factor = mass / (wave - middle)
    star_energy = factor * (energy / dens + (middle - u) * (middle + press / mass))
    flux = [flow + jnp.where(in_star, wave * (factor - dens), 0.0)]
    for k in (1, 2, 3):
        base = flow * vel[k] + press if k == normal else flow * vel[k]
        star = factor * (middle if k == normal else vel[k])
        flux.append(base + jnp.where(in_star, wave * (star - dens * vel[k]), 0.0))
    flux.append(u * (energy + press) + jnp.where(in_star, wave * (star_energy - energy), 0.0))
    return flux


def shifted_flux(prims, normal, shift):
    left, right = [], []
    for v in prims:
        d = shift(v, 1) - v
        upper, lower = edge_values(v, shift(d, -2), shift(d, -1), d, shift(d, 1))
        left.append(upper)
        right.append(shift(lower, 1))
    return hllc(left, right, normal)


def roll(v, step, axis):
    return pltpu.roll(v, step % v.shape[axis], axis)


def fine_entries(width):
    found = []
    for way, distance in enumerate((width - 1, 1 - width, -width, width)):
        for slot in range(2):
            shift, other = divmod(slot + distance, 3)
            if other < 2:
                found.append((way, slot, shift, other))
    return found


def fine_kernel(
    width,
    start_ref,
    side_ref,
    top_ref,
    code_ref,
    cur_ref,
    reg_x_ref,
    reg_z_ref,
    base_ref,
    slab_x,
    slab_z,
    got_x,
    got_z,
    send_sem,
    recv_sem,
):
    here = lax.axis_index("wide")
    deep = lax.axis_index("deep")
    entries = fine_entries(width)
    edge, cells = cur_ref.shape[2:]
    lanes = slab_z.shape[4]
    shifts = sorted({e[2] % width for e in entries} | {-e[2] % width for e in entries})
    barrier = pltpu.get_barrier_semaphore()
    for shift in shifts:
        pl.semaphore_signal(
            barrier,
            inc=1,
            device_id=(lax.rem(here + shift, width), deep),
            device_id_type=pl.DeviceIdType.MESH,
        )
    cur_ref[...] = start_ref[...]
    base_ref[...] = start_ref[...]
    reg_x_ref[...] = jnp.zeros_like(reg_x_ref)
    reg_z_ref[...] = jnp.zeros_like(reg_z_ref)
    pl.semaphore_wait(barrier, len(shifts))

    def shift_y(v, k):
        step = k % edge
        ypos = lax.broadcasted_iota(jnp.int32, v.shape, 1) % edge
        return jnp.where(ypos < edge - step, roll(v, -step, 1), roll(v, edge - step, 1))

    def copies(stage):
        made = []
        counts = [0, 0]
        for number, (way, slot, shift, other) in enumerate(entries):
            kind = way // 2
            source = (slab_x, slab_z)[kind].at[other, 1 if way in (0, 2) else 0]
            target = (got_x, got_z)[kind].at[stage, counts[kind]]
            counts[kind] += 1
            made.append(
                pltpu.make_async_remote_copy(
                    src_ref=source,
                    dst_ref=target,
                    send_sem=send_sem.at[number],
                    recv_sem=recv_sem.at[stage, number],
                    device_id=(lax.rem(here + (-shift % width), width), deep),
                    device_id_type=pl.DeviceIdType.MESH,
                )
            )
        return made

    def one_stage(stage, carry):
        odd = stage % 2 == 1
        theta = 0.5 * ((stage + 1) // 2).astype(jnp.float32)
        for slot in range(2):
            for k in range(5):
                v = cur_ref[slot, k]
                slab_x[slot, 0, k] = v[:8]
                slab_x[slot, 1, k] = roll(v, 3, 0)[:8]
                slab_z[slot, 0, k] = v[:, :lanes]
                slab_z[slot, 1, k] = roll(v, 3 * edge, 1)[:, :lanes]
        sends = copies(stage)
        for copy in sends:
            copy.start()
        changes = []
        for slot in range(2):
            flux = shifted_flux(primitive([cur_ref[slot, k] for k in range(5)]), 2, shift_y)
            changes.append([f - shift_y(f, -1) for f in flux])
        for copy in sends:
            copy.wait_recv()

        def ghost(slot, way, k):
            code = code_ref[slot, way]
            kind, side = divmod(way, 2)
            rim = (side_ref, top_ref)[kind]
            value = (1.0 - theta) * rim[slot, 0, side, k] + theta * rim[slot, 1, side, k]
            same = [e for e in entries if e[0] // 2 == kind]
            for index, entry in enumerate(same):
                if entry[0] == way and entry[1] == slot:
                    value = jnp.where(code == 1, (got_x, got_z)[kind][stage, index, k], value)
            if (slot, way) == (1, 0):
                value = jnp.where(code == 2, slab_x[0, 1, k], value)
            if (slot, way) == (0, 1):
                value = jnp.where(code == 2, slab_x[1, 0, k], value)
            return value

        for slot in range(2):
            change = changes[slot]
            padded = []
            for k in range(5):
                v = cur_ref[slot, k]
                centre = roll(jnp.concatenate([v, v[:8]], axis=0), 3, 0)
                low = ghost(slot, 0, k)
                rim = jnp.concatenate([low, low, roll(ghost(slot, 1, k), 3, 0)], axis=0)
                row = lax.broadcasted_iota(jnp.int32, rim.shape, 0)
                outer = (row < 3) | ((row >= edge + 3) & (row < edge + 6))
                padded.append(jnp.where(outer, rim, centre))
            flux = shifted_flux(primitive(padded), 1, lambda v, k: roll(v, -k, 0))
            for k in range(5):
                reg_x_ref[slot, 0, k] += flux[k][:8]
                reg_x_ref[slot, 1, k] += flux[k][edge:]
                change[k] = change[k] + roll(flux[k] - roll(flux[k], 1, 0), -3, 0)[:edge]
            padded = []
            for k in range(5):
                v = cur_ref[slot, k]
                centre = roll(jnp.concatenate([v, v[:, :lanes]], axis=1), 3 * edge, 1)
                low = ghost(slot, 2, k)
                fill = [low] * (cells // lanes)
                rim = jnp.concatenate(fill + [roll(ghost(slot, 3, k), 3 * edge, 1)], axis=1)
                lane = lax.broadcasted_iota(jnp.int32, rim.shape, 1)
                outer = (lane < 3 * edge) | (
                    (lane >= cells + 3 * edge) & (lane < cells + 6 * edge)
                )
                padded.append(jnp.where(outer, rim, centre))
            flux = shifted_flux(primitive(padded), 3, lambda v, k: roll(v, -k * edge, 1))
            for k in range(5):
                reg_z_ref[slot, 0, k] += flux[k][:, :lanes]
                reg_z_ref[slot, 1, k] += flux[k][:, cells:]
                total = change[k] + roll(flux[k] - roll(flux[k], edge, 1), -3 * edge, 1)[:, :cells]
                old = cur_ref[slot, k]
                base = jnp.where(odd, base_ref[slot, k], old)
                base_ref[slot, k] = base
                new = old - (fine_step / fine_spacing) * total
                cur_ref[slot, k] = jnp.where(odd, 0.5 * (base + new), new)
        for copy in sends:
            copy.wait_send()
        return carry

    lax.fori_loop(0, 4, one_stage, 0)


def fine_steps(width, start, side, top, codes):
    edge, cells = start.shape[2:]
    lanes = top.shape[5]
    entries = fine_entries(width)
    n_x = sum(e[0] < 2 for e in entries)
    vmem = pl.BlockSpec(memory_space=pltpu.VMEM)
    shape_x, shape_z = (5, 8, cells), (5, edge, lanes)
    return pl.pallas_call(
        partial(fine_kernel, width),
        in_specs=[vmem, vmem, vmem, pl.BlockSpec(memory_space=pltpu.SMEM)],
        out_specs=[vmem] * 3,
        out_shape=[
            jax.ShapeDtypeStruct(s, jnp.float32)
            for s in (start.shape, (2, 2) + shape_x, (2, 2) + shape_z)
        ],
        scratch_shapes=[
            pltpu.VMEM(start.shape, jnp.float32),
            pltpu.VMEM((2, 2) + shape_x, jnp.float32),
            pltpu.VMEM((2, 2) + shape_z, jnp.float32),
            pltpu.VMEM((4, n_x) + shape_x, jnp.float32),
            pltpu.VMEM((4, len(entries) - n_x) + shape_z, jnp.float32),
            pltpu.SemaphoreType.DMA((len(entries),)),
            pltpu.SemaphoreType.DMA((4, len(entries))),
        ],
        compiler_params=pltpu.CompilerParams(collective_id=0, has_side_effects=True),
    )(start, side, top, codes)


def coarse_kernel(second, base_ref, cur_ref, ghost_ref, out_ref, fx_ref, fz_ref):
    block = cur_ref.shape[1]
    left, right = [], []
    whole = [
        jnp.concatenate([ghost_ref[k, :3], cur_ref[k], ghost_ref[k, 3:]], axis=0) for k in range(5)
    ]
    for v in primitive(whole):
        d = v[1:] - v[:-1]
        n = block + 2
        upper, lower = edge_values(v[2 : 2 + n], d[:n], d[1 : 1 + n], d[2 : 2 + n], d[3 : 3 + n])
        left.append(upper[:-1])
        right.append(lower[1:])
    flux = hllc(left, right, 1)
    for k in range(5):
        fx_ref[k, 0] = flux[k][0]
        fx_ref[k, 1] = flux[k][block]
        out_ref[k] = flux[k][1:] - flux[k][:-1]
    prims = primitive([cur_ref[k] for k in range(5)])
    flux = shifted_flux(prims, 2, lambda v, k: roll(v, -k, 1))
    for k in range(5):
        out_ref[k] += flux[k] - roll(flux[k], 1, 1)
    prims = primitive([cur_ref[k] for k in range(5)])
    flux = shifted_flux(prims, 3, lambda v, k: roll(v, -k, 2))
    for k in range(5):
        fz_ref[k] = flux[k]
        change = out_ref[k] + flux[k] - roll(flux[k], 1, 2)
        new = cur_ref[k] - coarse_step * change
        out_ref[k] = 0.5 * (base_ref[k] + new) if second else new


def coarse_stage(second, base, state, layers, below, above):
    depth = state.shape[3]
    lanes = -(-(depth + 6) // 128) * 128
    cur = jnp.concatenate([below, state, above, state[..., : lanes - depth - 6]], axis=3)
    wide = [(0, 0, 0)] * 3 + [(3, lanes - depth - 3, 0)]
    one = jnp.float32(1.0)
    ghost = lax.pad(layers, one, wide)
    base = lax.pad(base, one, wide)
    shapes = [cur.shape, (5, 2) + cur.shape[2:], cur.shape]
    out, fx, fz = pl.pallas_call(
        partial(coarse_kernel, second),
        out_shape=[jax.ShapeDtypeStruct(s, jnp.float32) for s in shapes],
        interpret=INTERPRET,
    )(base, cur, ghost)
    return out[..., 3 : 3 + depth], fx[..., 3 : 3 + depth], fz[..., 2 : 3 + depth]


def ring(count):
    up = [(i, (i + 1) % count) for i in range(count)]
    return up, [(j, i) for i, j in up]


def halo(shard, axis, dim, width):
    up, down = ring(lax.axis_size(axis))
    length = shard.shape[dim]
    before = lax.ppermute(lax.slice_in_dim(shard, length - width, length, axis=dim), axis, up)
    after = lax.ppermute(lax.slice_in_dim(shard, 0, width, axis=dim), axis, down)
    return before, after


def mark(flag):
    return flag[:, None, None, None]


def select(flags, values):
    which = jnp.sum(
        flags.astype(jnp.int32) * jnp.arange(flags.shape[1], dtype=jnp.int32)[None], axis=1
    )
    return values[which]


def exchange(values):
    return lax.all_to_all(values, "wide", split_axis=0, concat_axis=0, tiled=True)


def spread_matrices(block):
    edge = 2 * block
    fine = np.arange(edge)
    face = np.zeros((block, block, edge, edge), np.float32)
    face[fine[None] // 2, fine[:, None] // 2, fine[:, None], fine[None]] = 1.0
    face = face.reshape(block * block, edge * edge)
    lanes = -(-3 * edge // 128) * 128
    top = np.zeros((block, 4, 2, lanes), np.float32)
    for side, chosen in enumerate(([0, 1, 1], [2, 2, 3])):
        for layer, source in enumerate(chosen):
            top[fine // 2, source, side, layer * edge + fine] = 1.0
    return face, top.reshape(4 * block, 2 * lanes)


def local(
    coarse_density,
    coarse_velocity,
    coarse_pressure,
    fine_density,
    fine_velocity,
    fine_pressure,
    patch_count,
    region_start,
):
    width = lax.axis_size("wide")
    here = lax.axis_index("wide")
    block = coarse_density.shape[0]
    depth = coarse_density.shape[2]
    places = depth // block - 2
    slots = fine_density.shape[1]
    edge = 2 * block
    cells = edge * edge
    blocks_all = width * places
    counts = patch_count[0]
    ends = jnp.cumsum(counts)
    begins = ends - counts
    total = ends[-1]
    anchor = region_start[0]
    face_matrix, top_matrix = spread_matrices(block)

    def locate(target):
        offset = (target - anchor) % blocks_all
        part = offset % 3
        rank = 2 * (offset // 3) + part
        live = (part < 2) & (rank < total)
        return live, jnp.minimum(offset // 3, width - 1)

    dest = jnp.arange(width, dtype=jnp.int32)
    pair = jnp.arange(2, dtype=jnp.int32)

    density = fine_density[0]
    velocity = fine_velocity[0]
    pressure = fine_pressure[0]
    initial = jnp.moveaxis(
        conserved(jnp.stack([density, velocity[:, 0], velocity[:, 1], velocity[:, 2], pressure])),
        0,
        1,
    )
    wanted = jnp.clip(2 * dest[:, None] + pair[None] - begins[here], 0, slots - 1)
    moved = exchange(initial[wanted])
    my_rank = 2 * here + pair
    holder = jnp.minimum(
        jnp.sum((my_rank[:, None] >= ends[None]).astype(jnp.int32), axis=1), width - 1
    )

    coarse = conserved(
        jnp.stack(
            [
                coarse_density,
                coarse_velocity[0],
                coarse_velocity[1],
                coarse_velocity[2],
                coarse_pressure,
            ]
        )
    )
    old_xl, old_xh = halo(coarse, "wide", 1, 3)
    zl, zh = halo(coarse, "deep", 3, 3)
    middle, early_x, early_z = coarse_stage(
        False, coarse, coarse, jnp.concatenate([old_xl, old_xh], axis=1), zl, zh
    )
    xl, xh = halo(middle, "wide", 1, 3)
    zl, zh = halo(middle, "deep", 3, 3)
    updated, later_x, later_z = coarse_stage(
        True, coarse, middle, jnp.concatenate([xl, xh], axis=1), zl, zh
    )
    mean_x = 0.5 * (early_x + later_x)
    mean_z = 0.5 * (early_z + later_z)
    new_xl, new_xh = halo(updated, "wide", 1, 2)

    def side_items(low, high):
        side = jnp.concatenate([low[:, -2:], high[:, :2]], axis=1)
        cut = side[..., block : block * (places + 1)].reshape(5, 4, block, places, block)
        return jnp.moveaxis(cut, 3, 0).reshape(places, -1)

    def top_items(state):
        blocked = state.reshape(5, block, block, places + 2, block)
        cut = jnp.concatenate([blocked[..., :-2, -2:], blocked[..., 2:, :2]], axis=-1)
        return jnp.moveaxis(cut, 3, 0).reshape(places, -1)

    items = jnp.concatenate(
        [side_items(old_xl, old_xh), side_items(new_xl, new_xh), top_items(coarse), top_items(updated)],
        axis=1,
    ).reshape(places, -1, 128)
    items, moved = lax.optimization_barrier((items, moved))
    start = jnp.stack([moved[holder[0], 0], moved[holder[1], 1]])
    height_ids = jnp.arange(places, dtype=jnp.int32)
    local_ident = height_ids * width + here
    live_here, device_here = locate(local_ident)
    to_device = live_here[None] & (device_here[None] == dest[:, None])
    received = exchange(select(to_device, items))

    my_ident = (anchor + 3 * here + pair) % blocks_all
    my_column = my_ident % width
    my_height = my_ident // width
    rims = received[my_column].reshape(2, 4, 5, -1)
    side_rims = rims[:, :2].reshape(2, 2, 5, 4, block * block)
    spread = jnp.dot(side_rims, face_matrix, precision=HIGHEST)
    filler = jnp.zeros(spread.shape[:3] + (5, cells), jnp.float32)
    side_ghosts = jnp.stack(
        [
            jnp.concatenate([spread[:, :, :, :2], spread[:, :, :, 1:2], filler], axis=3),
            jnp.concatenate([spread[:, :, :, 2:3], spread[:, :, :, 2:], filler], axis=3),
        ],
        axis=2,
    )
    top_rims = rims[:, 2:].reshape(2, 2, 5, block, 4 * block)
    top_ghosts = jnp.repeat(jnp.dot(top_rims, top_matrix, precision=HIGHEST), 2, axis=3)
    lanes = top_ghosts.shape[4] // 2
    top_ghosts = jnp.stack([top_ghosts[..., :lanes], top_ghosts[..., lanes:]], axis=2)

    wrap_low = my_column == 0
    wrap_high = my_column == width - 1
    row_ident = my_height * width
    live_xl = locate(row_ident + (my_column + width - 1) % width)[0]
    live_xh = locate(row_ident + (my_column + 1) % width)[0]
    live_zl = locate(my_ident - width)[0] & (my_height > 0)
    live_zh = locate(my_ident + width)[0] & (my_height < places - 1)

    codes = jnp.stack(
        [
            jnp.where(live_xl, jnp.where(wrap_low, 1, 2), 0),
            jnp.where(live_xh, jnp.where(wrap_high, 1, 2), 0),
            jnp.where(live_zl, 1, 0),
            jnp.where(live_zh, 1, 0),
        ],
        axis=1,
    ).astype(jnp.int32)
    states, reg_x, reg_z = fine_steps(width, start, side_ghosts, top_ghosts, codes)

    back = exchange(jnp.broadcast_to(states[None], (width,) + states.shape))
    slot_ids = jnp.arange(slots, dtype=jnp.int32)
    my_alive = slot_ids < counts[here]
    serial = jnp.clip(begins[here] + slot_ids, 0, 2 * width - 1)
    final_fine = back.reshape((2 * width,) + back.shape[2:])[serial]
    fine_out = jnp.where(mark(my_alive), final_fine, initial)[None]

    face_mean = face_matrix.T * 0.25
    side_regs = jnp.dot(
        reg_x[:, :, :, 2], face_mean * (0.5 * fine_step), precision=HIGHEST
    )
    tops = reg_z[..., 2 * edge : 3 * edge].reshape(2, 2, 5, block, 2, edge).sum(axis=4)
    half = np.repeat(np.eye(block, dtype=np.float32), 2, axis=0) * (0.25 * 0.5 * fine_step)
    top_regs = jnp.dot(tops, half, precision=HIGHEST)
    pooled = states.reshape(2, 5, block, 2, cells).sum(axis=3)
    averaged = jnp.dot(pooled, face_mean * 0.5, precision=HIGHEST)
    package = jnp.concatenate(
        [averaged.reshape(2, -1), side_regs.reshape(2, -1), top_regs.reshape(2, -1)], axis=1
    ).reshape(2, -1, 128)
    to_brick = my_column[None] == dest[:, None]
    brought = exchange(select(to_brick, package))
    picked = brought[device_here].reshape(places, -1)
    cube = 5 * block * block * block
    avg_here = picked[:, :cube].reshape(places, 5, block, block, block)
    regs_here = picked[:, cube:].reshape(places, 4, 5, block, block)
    edge_xl = live_here & ~locate(height_ids * width + (here + width - 1) % width)[0]
    edge_xh = live_here & ~locate(height_ids * width + (here + 1) % width)[0]
    edge_zl = live_here & ~(locate(local_ident - width)[0] & (height_ids > 0))
    edge_zh = live_here & ~(locate(local_ident + width)[0] & (height_ids < places - 1))
    span = slice(block, block * (places + 1))

    def along_z(term):
        return jnp.moveaxis(term, 0, 2).reshape(5, block, places * block)

    low_mid = jnp.where(
        jnp.repeat(edge_xl, block),
        coarse_step * mean_x[:, 0, :, span] - along_z(regs_here[:, 0]),
        0.0,
    )
    high_mid = jnp.where(
        jnp.repeat(edge_xh, block),
        -(coarse_step * mean_x[:, 1, :, span] - along_z(regs_here[:, 1])),
        0.0,
    )
    up, down = ring(width)
    to_first = lax.ppermute(high_mid, "wide", up)
    to_last = lax.ppermute(low_mid, "wide", down)
    under = mean_z[..., :depth].reshape(5, block, block, places + 2, block)[..., 0]
    low_terms = coarse_step * under[..., 1:-1] - jnp.moveaxis(regs_here[:, 2], 0, 3)
    high_terms = coarse_step * under[..., 2:] - jnp.moveaxis(regs_here[:, 3], 0, 3)
    low_terms = jnp.where(edge_zl, low_terms, 0.0)
    high_terms = jnp.where(edge_zh, -high_terms, 0.0)
    none = ((0, 0),) * 3
    last_cell = jnp.pad(low_terms, none + ((0, 2),))[..., None]
    first_cell = jnp.pad(high_terms, none + ((2, 0),))[..., None]
    in_block = jnp.arange(block)
    correction = jnp.where(in_block == block - 1, last_cell, 0.0) + jnp.where(
        in_block == 0, first_cell, 0.0
    )
    result = updated + correction.reshape(updated.shape)
    ends_z = ((0, 0), (0, 0), (block, block))
    layer = jnp.arange(block)[None, :, None, None]
    result = result + jnp.where(layer == 0, jnp.pad(to_first, ends_z)[:, None], 0.0)
    result = result + jnp.where(layer == block - 1, jnp.pad(to_last, ends_z)[:, None], 0.0)
    avg_z = jnp.moveaxis(avg_here, 0, 3).reshape(5, block, block, places * block)
    avg_z = jnp.pad(avg_z, none + ((block, block),))
    covered = jnp.pad(jnp.repeat(live_here, block), (block, block))
    return jnp.where(covered, avg_z, result), fine_out


def solution(mesh):
    return jax.shard_map(
        local,
        mesh=mesh,
        in_specs=(
            P("wide", None, "deep"),
            P(None, "wide", None, "deep"),
            P("wide", None, "deep"),
            P("deep", "wide", None, None),
            P("deep", "wide", None, None, None),
            P("deep", "wide", None, None),
            P("deep", None),
            P("deep"),
        ),
        out_specs=(P(None, "wide", None, "deep"), P("deep", "wide", None, None, None)),
        check_vma=False,
    )
```

```python
from functools import partial

import jax
import jax.numpy as jnp
import numpy as np
from jax import lax
from jax.experimental import pallas as pl
from jax.experimental.pallas import tpu as pltpu
from jax.sharding import PartitionSpec as P

heat_ratio = 1.4
weno_floor = 1e-06
coarse_step = 0.2
fine_step = 0.1
fine_spacing = 0.5
INTERPRET = False
HIGHEST = lax.Precision.HIGHEST


def primitive(state):
    density = state[0]
    speed_x = state[1] / density
    speed_y = state[2] / density
    speed_z = state[3] / density
    kinetic = 0.5 * density * (speed_x * speed_x + speed_y * speed_y + speed_z * speed_z)
    pressure = (heat_ratio - 1.0) * (state[4] - kinetic)
    return [density, speed_x, speed_y, speed_z, pressure]


def conserved(prims):
    density = prims[0]
    kinetic = 0.5 * density * (prims[1] * prims[1] + prims[2] * prims[2] + prims[3] * prims[3])
    energy = prims[4] / (heat_ratio - 1.0) + kinetic
    return jnp.stack([density, density * prims[1], density * prims[2], density * prims[3], energy])


def edge_values(v, e1, e2, e3, e4):
    s1, s2, s3 = e2 - e1, e3 - e2, e4 - e3
    t1, t2, t3 = 3.0 * e2 - e1, e2 + e3, 3.0 * e3 - e4
    b1 = weno_floor + (13.0 / 12.0) * (s1 * s1) + 0.25 * (t1 * t1)
    b2 = weno_floor + (13.0 / 12.0) * (s2 * s2) + 0.25 * (t2 * t2)
    b3 = weno_floor + (13.0 / 12.0) * (s3 * s3) + 0.25 * (t3 * t3)
    q1, q2, q3 = b1 * b1, b2 * b2, b3 * b3
    a = q2 * q3
    b = 6.0 * (q1 * q3)
    c = q1 * q2
    a3, c3 = 3.0 * a, 3.0 * c
    upper = v + (a * (5.0 * e2 - 2.0 * e1) + b * (e2 + 2.0 * e3) + c3 * (4.0 * e3 - e4)) / (
        6.0 * (a + b + c3)
    )
    lower = v - (c * (5.0 * e3 - 2.0 * e4) + b * (e3 + 2.0 * e2) + a3 * (4.0 * e2 - e1)) / (
        6.0 * (c + b + a3)
    )
    return upper, lower


def hllc(left, right, normal):
    rl, ul, pl_ = left[0], left[normal], left[4]
    rr, ur, pr = right[0], right[normal], right[4]
    sound_left = jnp.sqrt(heat_ratio * pl_ / rl)
    sound_right = jnp.sqrt(heat_ratio * pr / rr)
    slow = jnp.minimum(ul - sound_left, ur - sound_right)
    fast = jnp.maximum(ul + sound_left, ur + sound_right)
    mass_left = rl * (slow - ul)
    mass_right = rr * (fast - ur)
    middle = (pr - pl_ + mass_left * ul - mass_right * ur) / (mass_left - mass_right)
    use_left = (slow >= 0.0) | (middle >= 0.0)
    dens = jnp.where(use_left, rl, rr)
    vel = [None] + [jnp.where(use_left, left[k], right[k]) for k in (1, 2, 3)]
    press = jnp.where(use_left, pl_, pr)
    mass = jnp.where(use_left, mass_left, mass_right)
    wave = jnp.where(use_left, slow, fast)
    in_star = (use_left & (slow < 0.0)) | (jnp.logical_not(use_left) & (fast > 0.0))
    u = vel[normal]
    energy = press / (heat_ratio - 1.0) + 0.5 * dens * (
        vel[1] * vel[1] + vel[2] * vel[2] + vel[3] * vel[3]
    )
    flow = dens * u
    factor = mass / (wave - middle)
    star_energy = factor * (energy / dens + (middle - u) * (middle + press / mass))
    flux = [flow + jnp.where(in_star, wave * (factor - dens), 0.0)]
    for k in (1, 2, 3):
        base = flow * vel[k] + press if k == normal else flow * vel[k]
        star = factor * (middle if k == normal else vel[k])
        flux.append(base + jnp.where(in_star, wave * (star - dens * vel[k]), 0.0))
    flux.append(u * (energy + press) + jnp.where(in_star, wave * (star_energy - energy), 0.0))
    return flux


def shifted_flux(prims, normal, shift):
    left, right = [], []
    for v in prims:
        d = shift(v, 1) - v
        upper, lower = edge_values(v, shift(d, -2), shift(d, -1), d, shift(d, 1))
        left.append(upper)
        right.append(shift(lower, 1))
    return hllc(left, right, normal)


def roll(v, step, axis):
    return pltpu.roll(v, step % v.shape[axis], axis)


def fine_entries(width):
    found = []
    for way, distance in enumerate((width - 1, 1 - width, -width, width)):
        for slot in range(2):
            shift, other = divmod(slot + distance, 3)
            if other < 2:
                found.append((way, slot, shift, other))
    return found


def fine_kernel(
    width,
    start_ref,
    side_ref,
    top_ref,
    code_ref,
    cur_ref,
    reg_x_ref,
    reg_z_ref,
    base_ref,
    slab_x,
    slab_z,
    got_x,
    got_z,
    send_sem,
    recv_sem,
):
    here = lax.axis_index("wide")
    deep = lax.axis_index("deep")
    entries = fine_entries(width)
    edge, cells = cur_ref.shape[2:]
    lanes = slab_z.shape[4]
    shifts = sorted({e[2] % width for e in entries} | {-e[2] % width for e in entries})
    barrier = pltpu.get_barrier_semaphore()
    for shift in shifts:
        pl.semaphore_signal(
            barrier,
            inc=1,
            device_id=(lax.rem(here + shift, width), deep),
            device_id_type=pl.DeviceIdType.MESH,
        )
    cur_ref[...] = start_ref[...]
    base_ref[...] = start_ref[...]
    reg_x_ref[...] = jnp.zeros_like(reg_x_ref)
    reg_z_ref[...] = jnp.zeros_like(reg_z_ref)
    pl.semaphore_wait(barrier, len(shifts))

    def shift_y(v, k):
        step = k % edge
        ypos = lax.broadcasted_iota(jnp.int32, v.shape, 1) % edge
        return jnp.where(ypos < edge - step, roll(v, -step, 1), roll(v, edge - step, 1))

    def copies(stage):
        made = []
        counts = [0, 0]
        for number, (way, slot, shift, other) in enumerate(entries):
            kind = way // 2
            source = (slab_x, slab_z)[kind].at[other, 1 if way in (0, 2) else 0]
            target = (got_x, got_z)[kind].at[stage, counts[kind]]
            counts[kind] += 1
            made.append(
                pltpu.make_async_remote_copy(
                    src_ref=source,
                    dst_ref=target,
                    send_sem=send_sem.at[number],
                    recv_sem=recv_sem.at[stage, number],
                    device_id=(lax.rem(here + (-shift % width), width), deep),
                    device_id_type=pl.DeviceIdType.MESH,
                )
            )
        return made

    def one_stage(stage, carry):
        odd = stage % 2 == 1
        theta = 0.5 * ((stage + 1) // 2).astype(jnp.float32)
        for slot in range(2):
            for k in range(5):
                v = cur_ref[slot, k]
                slab_x[slot, 0, k] = v[:8]
                slab_x[slot, 1, k] = roll(v, 3, 0)[:8]
                slab_z[slot, 0, k] = v[:, :lanes]
                slab_z[slot, 1, k] = roll(v, 3 * edge, 1)[:, :lanes]
        sends = copies(stage)
        for copy in sends:
            copy.start()
        changes = []
        for slot in range(2):
            flux = shifted_flux(primitive([cur_ref[slot, k] for k in range(5)]), 2, shift_y)
            changes.append([f - shift_y(f, -1) for f in flux])
        for copy in sends:
            copy.wait_recv()

        def ghost(slot, way, k):
            code = code_ref[slot, way]
            kind, side = divmod(way, 2)
            rim = (side_ref, top_ref)[kind]
            value = (1.0 - theta) * rim[slot, 0, side, k] + theta * rim[slot, 1, side, k]
            same = [e for e in entries if e[0] // 2 == kind]
            for index, entry in enumerate(same):
                if entry[0] == way and entry[1] == slot:
                    value = jnp.where(code == 1, (got_x, got_z)[kind][stage, index, k], value)
            if (slot, way) == (1, 0):
                value = jnp.where(code == 2, slab_x[0, 1, k], value)
            if (slot, way) == (0, 1):
                value = jnp.where(code == 2, slab_x[1, 0, k], value)
            return value

        for slot in range(2):
            change = changes[slot]
            padded = []
            for k in range(5):
                v = cur_ref[slot, k]
                centre = roll(jnp.concatenate([v, v[:8]], axis=0), 3, 0)
                low = ghost(slot, 0, k)
                rim = jnp.concatenate([low, low, roll(ghost(slot, 1, k), 3, 0)], axis=0)
                row = lax.broadcasted_iota(jnp.int32, rim.shape, 0)
                outer = (row < 3) | ((row >= edge + 3) & (row < edge + 6))
                padded.append(jnp.where(outer, rim, centre))
            flux = shifted_flux(primitive(padded), 1, lambda v, k: roll(v, -k, 0))
            for k in range(5):
                reg_x_ref[slot, 0, k] += flux[k][:8]
                reg_x_ref[slot, 1, k] += flux[k][edge:]
                change[k] = change[k] + roll(flux[k] - roll(flux[k], 1, 0), -3, 0)[:edge]
            padded = []
            for k in range(5):
                v = cur_ref[slot, k]
                centre = roll(jnp.concatenate([v, v[:, :lanes]], axis=1), 3 * edge, 1)
                low = ghost(slot, 2, k)
                fill = [low] * (cells // lanes)
                rim = jnp.concatenate(fill + [roll(ghost(slot, 3, k), 3 * edge, 1)], axis=1)
                lane = lax.broadcasted_iota(jnp.int32, rim.shape, 1)
                outer = (lane < 3 * edge) | (
                    (lane >= cells + 3 * edge) & (lane < cells + 6 * edge)
                )
                padded.append(jnp.where(outer, rim, centre))
            flux = shifted_flux(primitive(padded), 3, lambda v, k: roll(v, -k * edge, 1))
            for k in range(5):
                reg_z_ref[slot, 0, k] += flux[k][:, :lanes]
                reg_z_ref[slot, 1, k] += flux[k][:, cells:]
                total = change[k] + roll(flux[k] - roll(flux[k], edge, 1), -3 * edge, 1)[:, :cells]
                old = cur_ref[slot, k]
                base = jnp.where(odd, base_ref[slot, k], old)
                base_ref[slot, k] = base
                new = old - (fine_step / fine_spacing) * total
                cur_ref[slot, k] = jnp.where(odd, 0.5 * (base + new), new)
        for copy in sends:
            copy.wait_send()
        return carry

    lax.fori_loop(0, 4, one_stage, 0)


def fine_steps(width, start, side, top, codes):
    edge, cells = start.shape[2:]
    lanes = top.shape[5]
    entries = fine_entries(width)
    n_x = sum(e[0] < 2 for e in entries)
    vmem = pl.BlockSpec(memory_space=pltpu.VMEM)
    shape_x, shape_z = (5, 8, cells), (5, edge, lanes)
    return pl.pallas_call(
        partial(fine_kernel, width),
        in_specs=[vmem, vmem, vmem, pl.BlockSpec(memory_space=pltpu.SMEM)],
        out_specs=[vmem] * 3,
        out_shape=[
            jax.ShapeDtypeStruct(s, jnp.float32)
            for s in (start.shape, (2, 2) + shape_x, (2, 2) + shape_z)
        ],
        scratch_shapes=[
            pltpu.VMEM(start.shape, jnp.float32),
            pltpu.VMEM((2, 2) + shape_x, jnp.float32),
            pltpu.VMEM((2, 2) + shape_z, jnp.float32),
            pltpu.VMEM((4, n_x) + shape_x, jnp.float32),
            pltpu.VMEM((4, len(entries) - n_x) + shape_z, jnp.float32),
            pltpu.SemaphoreType.DMA((len(entries),)),
            pltpu.SemaphoreType.DMA((4, len(entries))),
        ],
        compiler_params=pltpu.CompilerParams(collective_id=0, has_side_effects=True),
    )(start, side, top, codes)


def coarse_kernel(second, base_ref, cur_ref, ghost_ref, out_ref, fx_ref, fz_ref):
    block = cur_ref.shape[1]
    left, right = [], []
    whole = [
        jnp.concatenate([ghost_ref[k, :3], cur_ref[k], ghost_ref[k, 3:]], axis=0) for k in range(5)
    ]
    for v in primitive(whole):
        d = v[1:] - v[:-1]
        n = block + 2
        upper, lower = edge_values(v[2 : 2 + n], d[:n], d[1 : 1 + n], d[2 : 2 + n], d[3 : 3 + n])
        left.append(upper[:-1])
        right.append(lower[1:])
    flux = hllc(left, right, 1)
    for k in range(5):
        fx_ref[k, 0] = flux[k][0]
        fx_ref[k, 1] = flux[k][block]
        out_ref[k] = flux[k][1:] - flux[k][:-1]
    prims = primitive([cur_ref[k] for k in range(5)])
    flux = shifted_flux(prims, 2, lambda v, k: roll(v, -k, 1))
    for k in range(5):
        out_ref[k] += flux[k] - roll(flux[k], 1, 1)
    prims = primitive([cur_ref[k] for k in range(5)])
    flux = shifted_flux(prims, 3, lambda v, k: roll(v, -k, 2))
    for k in range(5):
        fz_ref[k] = flux[k]
        change = out_ref[k] + flux[k] - roll(flux[k], 1, 2)
        new = cur_ref[k] - coarse_step * change
        out_ref[k] = 0.5 * (base_ref[k] + new) if second else new


def coarse_stage(second, base, state, layers, below, above):
    depth = state.shape[3]
    lanes = -(-(depth + 6) // 128) * 128
    cur = jnp.concatenate([below, state, above, state[..., : lanes - depth - 6]], axis=3)
    wide = [(0, 0, 0)] * 3 + [(3, lanes - depth - 3, 0)]
    one = jnp.float32(1.0)
    ghost = lax.pad(layers, one, wide)
    base = lax.pad(base, one, wide)
    shapes = [cur.shape, (5, 2) + cur.shape[2:], cur.shape]
    out, fx, fz = pl.pallas_call(
        partial(coarse_kernel, second),
        out_shape=[jax.ShapeDtypeStruct(s, jnp.float32) for s in shapes],
        interpret=INTERPRET,
    )(base, cur, ghost)
    return out[..., 3 : 3 + depth], fx[..., 3 : 3 + depth], fz[..., 2 : 3 + depth]


def ring(count):
    up = [(i, (i + 1) % count) for i in range(count)]
    return up, [(j, i) for i, j in up]


def halo(shard, axis, dim, width):
    up, down = ring(lax.axis_size(axis))
    length = shard.shape[dim]
    before = lax.ppermute(lax.slice_in_dim(shard, length - width, length, axis=dim), axis, up)
    after = lax.ppermute(lax.slice_in_dim(shard, 0, width, axis=dim), axis, down)
    return before, after


def mark(flag):
    return flag[:, None, None, None]


def select(flags, values):
    which = jnp.sum(
        flags.astype(jnp.int32) * jnp.arange(flags.shape[1], dtype=jnp.int32)[None], axis=1
    )
    return values[which]


def exchange(values):
    return lax.all_to_all(values, "wide", split_axis=0, concat_axis=0, tiled=True)


def spread_matrices(block):
    edge = 2 * block
    fine = np.arange(edge)
    face = np.zeros((block, block, edge, edge), np.float32)
    face[fine[None] // 2, fine[:, None] // 2, fine[:, None], fine[None]] = 1.0
    face = face.reshape(block * block, edge * edge)
    lanes = -(-3 * edge // 128) * 128
    top = np.zeros((block, 4, 2, lanes), np.float32)
    for side, chosen in enumerate(([0, 1, 1], [2, 2, 3])):
        for layer, source in enumerate(chosen):
            top[fine // 2, source, side, layer * edge + fine] = 1.0
    return face, top.reshape(4 * block, 2 * lanes)


def local(
    coarse_density,
    coarse_velocity,
    coarse_pressure,
    fine_density,
    fine_velocity,
    fine_pressure,
    patch_count,
    region_start,
):
    width = lax.axis_size("wide")
    here = lax.axis_index("wide")
    block = coarse_density.shape[0]
    depth = coarse_density.shape[2]
    places = depth // block - 2
    slots = fine_density.shape[1]
    edge = 2 * block
    cells = edge * edge
    blocks_all = width * places
    counts = patch_count[0]
    ends = jnp.cumsum(counts)
    begins = ends - counts
    total = ends[-1]
    anchor = region_start[0]
    face_matrix, top_matrix = spread_matrices(block)

    def locate(target):
        offset = (target - anchor) % blocks_all
        part = offset % 3
        rank = 2 * (offset // 3) + part
        live = (part < 2) & (rank < total)
        return live, jnp.minimum(offset // 3, width - 1)

    dest = jnp.arange(width, dtype=jnp.int32)
    pair = jnp.arange(2, dtype=jnp.int32)

    density = fine_density[0]
    velocity = fine_velocity[0]
    pressure = fine_pressure[0]
    initial = jnp.moveaxis(
        conserved(jnp.stack([density, velocity[:, 0], velocity[:, 1], velocity[:, 2], pressure])),
        0,
        1,
    )
    wanted = jnp.clip(2 * dest[:, None] + pair[None] - begins[here], 0, slots - 1)
    moved = exchange(initial[wanted])
    my_rank = 2 * here + pair
    holder = jnp.minimum(
        jnp.sum((my_rank[:, None] >= ends[None]).astype(jnp.int32), axis=1), width - 1
    )

    coarse = conserved(
        jnp.stack(
            [
                coarse_density,
                coarse_velocity[0],
                coarse_velocity[1],
                coarse_velocity[2],
                coarse_pressure,
            ]
        )
    )
    old_xl, old_xh = halo(coarse, "wide", 1, 3)
    zl, zh = halo(coarse, "deep", 3, 3)
    middle, early_x, early_z = coarse_stage(
        False, coarse, coarse, jnp.concatenate([old_xl, old_xh], axis=1), zl, zh
    )
    xl, xh = halo(middle, "wide", 1, 3)
    zl, zh = halo(middle, "deep", 3, 3)
    updated, later_x, later_z = coarse_stage(
        True, coarse, middle, jnp.concatenate([xl, xh], axis=1), zl, zh
    )
    mean_x = 0.5 * (early_x + later_x)
    mean_z = 0.5 * (early_z + later_z)
    new_xl, new_xh = halo(updated, "wide", 1, 2)

    updated, moved = lax.optimization_barrier((updated, moved))
    start = jnp.stack([moved[holder[0], 0], moved[holder[1], 1]])
    height_ids = jnp.arange(places, dtype=jnp.int32)
    local_ident = height_ids * width + here
    live_here, device_here = locate(local_ident)
    to_device = live_here[None] & (device_here[None] == dest[:, None])
    bottom = block * (1 + jnp.sum(jnp.where(to_device, height_ids[None], 0), axis=1))
    cell_ids = jnp.arange(depth, dtype=jnp.int32)

    def one_hot(offsets, flags):
        found = cell_ids == (bottom[:, None] + np.array(offsets, np.int32))[..., None]
        return (found & flags[:, None, None]).astype(jnp.float32)

    inside = one_hot(range(block), jnp.any(to_device, axis=1))
    around = one_hot((-2, -1, block, block + 1), jnp.any(to_device, axis=1))
    sides = jnp.stack(
        [
            jnp.concatenate([low[:, -2:], high[:, :2]], axis=1)
            for low, high in ((old_xl, old_xh), (new_xl, new_xh))
        ]
    ).reshape(-1, depth)
    planes = jnp.stack([coarse, updated]).reshape(-1, depth)
    items = jnp.concatenate(
        [
            jnp.einsum("dzn,mn->dzm", inside, sides, precision=HIGHEST).reshape(width, -1),
            jnp.einsum("dln,mn->dlm", around, planes, precision=HIGHEST).reshape(width, -1),
        ],
        axis=1,
    )
    received = exchange(items.reshape(width, -1, 128))

    my_ident = (anchor + 3 * here + pair) % blocks_all
    my_column = my_ident % width
    my_height = my_ident // width
    rims = received[my_column].reshape(2, -1)
    side_rims = rims[:, : 40 * block * block].reshape(2, block, 2, 5, 4, block)
    top_rims = rims[:, 40 * block * block :].reshape(2, 4, 2, 5, block, block)
    face_rows = face_matrix.reshape(block, block, cells)
    spread = jnp.einsum("pztcly,yzn->ptcln", side_rims, face_rows, precision=HIGHEST)
    top_rows = top_matrix.reshape(block, 4, -1)
    top_spread = jnp.einsum("pltcxy,yln->ptcxn", top_rims, top_rows, precision=HIGHEST)
    filler = jnp.zeros(spread.shape[:3] + (5, cells), jnp.float32)
    side_ghosts = jnp.stack(
        [
            jnp.concatenate([spread[:, :, :, :2], spread[:, :, :, 1:2], filler], axis=3),
            jnp.concatenate([spread[:, :, :, 2:3], spread[:, :, :, 2:], filler], axis=3),
        ],
        axis=2,
    )
    top_ghosts = jnp.repeat(top_spread, 2, axis=3)
    lanes = top_ghosts.shape[4] // 2
    top_ghosts = jnp.stack([top_ghosts[..., :lanes], top_ghosts[..., lanes:]], axis=2)

    wrap_low = my_column == 0
    wrap_high = my_column == width - 1
    row_ident = my_height * width
    live_xl = locate(row_ident + (my_column + width - 1) % width)[0]
    live_xh = locate(row_ident + (my_column + 1) % width)[0]
    live_zl = locate(my_ident - width)[0] & (my_height > 0)
    live_zh = locate(my_ident + width)[0] & (my_height < places - 1)

    codes = jnp.stack(
        [
            jnp.where(live_xl, jnp.where(wrap_low, 1, 2), 0),
            jnp.where(live_xh, jnp.where(wrap_high, 1, 2), 0),
            jnp.where(live_zl, 1, 0),
            jnp.where(live_zh, 1, 0),
        ],
        axis=1,
    ).astype(jnp.int32)
    states, reg_x, reg_z = fine_steps(width, start, side_ghosts, top_ghosts, codes)

    back = exchange(jnp.broadcast_to(states[None], (width,) + states.shape))
    slot_ids = jnp.arange(slots, dtype=jnp.int32)
    my_alive = slot_ids < counts[here]
    serial = jnp.clip(begins[here] + slot_ids, 0, 2 * width - 1)
    final_fine = back.reshape((2 * width,) + back.shape[2:])[serial]
    fine_out = jnp.where(mark(my_alive), final_fine, initial)[None]

    face_mean = face_matrix.T * 0.25
    side_regs = jnp.dot(
        reg_x[:, :, :, 2], face_mean * (0.5 * fine_step), precision=HIGHEST
    )
    tops = reg_z[..., 2 * edge : 3 * edge].reshape(2, 2, 5, block, 2, edge).sum(axis=4)
    half = np.repeat(np.eye(block, dtype=np.float32), 2, axis=0) * (0.25 * 0.5 * fine_step)
    top_regs = jnp.dot(tops, half, precision=HIGHEST)
    pooled = states.reshape(2, 5, block, 2, cells).sum(axis=3)
    averaged = jnp.dot(pooled, face_mean * 0.5, precision=HIGHEST)
    averaged = averaged.reshape(2, 5, block, block, block)
    side_regs = side_regs.reshape(2, 2, 5, block, block)
    package = jnp.concatenate(
        [
            jnp.moveaxis(averaged, 4, 1).reshape(2, -1),
            top_regs.reshape(2, -1),
            jnp.moveaxis(side_regs, 4, 2).reshape(2, -1),
        ],
        axis=1,
    ).reshape(2, -1, 128)
    to_brick = my_column[None] == dest[:, None]
    brought = exchange(select(to_brick, package))
    brought = brought.reshape(width, -1)
    face = 5 * block * block
    main = brought[:, : (block + 2) * face].reshape(width, block + 2, face)
    side_part = brought[:, (block + 2) * face :].reshape(width, 2, block, 5 * block)
    edge_xl = live_here & ~locate(height_ids * width + (here + width - 1) % width)[0]
    edge_xh = live_here & ~locate(height_ids * width + (here + 1) % width)[0]
    edge_zl = live_here & ~(locate(local_ident - width)[0] & (height_ids > 0))
    edge_zh = live_here & ~(locate(local_ident + width)[0] & (height_ids < places - 1))

    def with_edge(flags):
        return jnp.any(to_device & flags[None], axis=1)

    def at_cells(flags, first, count):
        padded = jnp.pad(jnp.repeat(flags, block), (block, block))
        phase = cell_ids % block
        return padded & (phase >= first) & (phase < first + count)

    def side_terms(side, flags):
        chosen = inside * with_edge(flags)[:, None, None].astype(jnp.float32)
        term = jnp.einsum("dzm,dzn->mn", side_part[:, side], chosen, precision=HIGHEST)
        coarse_part = jnp.where(at_cells(flags, 0, block), coarse_step * mean_x[:, side], 0.0)
        return coarse_part - term.reshape(coarse_part.shape)

    up, down = ring(width)
    to_first = lax.ppermute(-side_terms(1, edge_xh), "wide", up)
    to_last = lax.ppermute(side_terms(0, edge_xl), "wide", down)
    rows = jnp.concatenate(
        [
            inside,
            -one_hot((-1,), with_edge(edge_zl)),
            one_hot((block,), with_edge(edge_zh)),
        ],
        axis=1,
    )
    placed = jnp.einsum("dkm,dkn->mn", main, rows, precision=HIGHEST).reshape(updated.shape)
    below_low = jnp.roll(at_cells(edge_zl, 0, 1), -1)
    above_high = jnp.roll(at_cells(edge_zh, block - 1, 1), 1)
    result = updated + jnp.where(below_low, coarse_step * mean_z[..., 1:], 0.0)
    result = result - jnp.where(above_high, coarse_step * mean_z[..., :-1], 0.0)
    layer = jnp.arange(block)[None, :, None, None]
    result = result + jnp.where(layer == 0, to_first[:, None], 0.0)
    result = result + jnp.where(layer == block - 1, to_last[:, None], 0.0)
    return jnp.where(at_cells(live_here, 0, block), 0.0, result) + placed, fine_out


def solution(mesh):
    return jax.shard_map(
        local,
        mesh=mesh,
        in_specs=(
            P("wide", None, "deep"),
            P(None, "wide", None, "deep"),
            P("wide", None, "deep"),
            P("deep", "wide", None, None),
            P("deep", "wide", None, None, None),
            P("deep", "wide", None, None),
            P("deep", None),
            P("deep"),
        ),
        out_specs=(P(None, "wide", None, "deep"), P("deep", "wide", None, None, None)),
        check_vma=False,
    )
```

```python
from functools import partial

import jax
import jax.numpy as jnp
import numpy as np
from jax import lax
from jax.experimental import pallas as pl
from jax.experimental.pallas import tpu as pltpu
from jax.sharding import PartitionSpec as P

heat_ratio = 1.4
weno_floor = 1e-06
coarse_step = 0.2
fine_step = 0.1
fine_spacing = 0.5
INTERPRET = False
HIGHEST = lax.Precision.HIGHEST


def primitive(state):
    density = state[0]
    speed_x = state[1] / density
    speed_y = state[2] / density
    speed_z = state[3] / density
    kinetic = 0.5 * density * (speed_x * speed_x + speed_y * speed_y + speed_z * speed_z)
    pressure = (heat_ratio - 1.0) * (state[4] - kinetic)
    return [density, speed_x, speed_y, speed_z, pressure]


def conserved(prims):
    density = prims[0]
    kinetic = 0.5 * density * (prims[1] * prims[1] + prims[2] * prims[2] + prims[3] * prims[3])
    energy = prims[4] / (heat_ratio - 1.0) + kinetic
    return jnp.stack([density, density * prims[1], density * prims[2], density * prims[3], energy])


def edge_values(v, e1, e2, e3, e4):
    s1, s2, s3 = e2 - e1, e3 - e2, e4 - e3
    t1, t2, t3 = 3.0 * e2 - e1, e2 + e3, 3.0 * e3 - e4
    b1 = weno_floor + (13.0 / 12.0) * (s1 * s1) + 0.25 * (t1 * t1)
    b2 = weno_floor + (13.0 / 12.0) * (s2 * s2) + 0.25 * (t2 * t2)
    b3 = weno_floor + (13.0 / 12.0) * (s3 * s3) + 0.25 * (t3 * t3)
    q1, q2, q3 = b1 * b1, b2 * b2, b3 * b3
    a = q2 * q3
    b = 6.0 * (q1 * q3)
    c = q1 * q2
    a3, c3 = 3.0 * a, 3.0 * c
    upper = v + (a * (5.0 * e2 - 2.0 * e1) + b * (e2 + 2.0 * e3) + c3 * (4.0 * e3 - e4)) / (
        6.0 * (a + b + c3)
    )
    lower = v - (c * (5.0 * e3 - 2.0 * e4) + b * (e3 + 2.0 * e2) + a3 * (4.0 * e2 - e1)) / (
        6.0 * (c + b + a3)
    )
    return upper, lower


def hllc(left, right, normal):
    rl, ul, pl_ = left[0], left[normal], left[4]
    rr, ur, pr = right[0], right[normal], right[4]
    sound_left = jnp.sqrt(heat_ratio * pl_ / rl)
    sound_right = jnp.sqrt(heat_ratio * pr / rr)
    slow = jnp.minimum(ul - sound_left, ur - sound_right)
    fast = jnp.maximum(ul + sound_left, ur + sound_right)
    mass_left = rl * (slow - ul)
    mass_right = rr * (fast - ur)
    middle = (pr - pl_ + mass_left * ul - mass_right * ur) / (mass_left - mass_right)
    use_left = (slow >= 0.0) | (middle >= 0.0)
    dens = jnp.where(use_left, rl, rr)
    vel = [None] + [jnp.where(use_left, left[k], right[k]) for k in (1, 2, 3)]
    press = jnp.where(use_left, pl_, pr)
    mass = jnp.where(use_left, mass_left, mass_right)
    wave = jnp.where(use_left, slow, fast)
    in_star = (use_left & (slow < 0.0)) | (jnp.logical_not(use_left) & (fast > 0.0))
    u = vel[normal]
    energy = press / (heat_ratio - 1.0) + 0.5 * dens * (
        vel[1] * vel[1] + vel[2] * vel[2] + vel[3] * vel[3]
    )
    flow = dens * u
    factor = mass / (wave - middle)
    star_energy = factor * (energy / dens + (middle - u) * (middle + press / mass))
    flux = [flow + jnp.where(in_star, wave * (factor - dens), 0.0)]
    for k in (1, 2, 3):
        base = flow * vel[k] + press if k == normal else flow * vel[k]
        star = factor * (middle if k == normal else vel[k])
        flux.append(base + jnp.where(in_star, wave * (star - dens * vel[k]), 0.0))
    flux.append(u * (energy + press) + jnp.where(in_star, wave * (star_energy - energy), 0.0))
    return flux


def shifted_flux(prims, normal, shift):
    left, right = [], []
    for v in prims:
        d = shift(v, 1) - v
        upper, lower = edge_values(v, shift(d, -2), shift(d, -1), d, shift(d, 1))
        left.append(upper)
        right.append(shift(lower, 1))
    return hllc(left, right, normal)


def roll(v, step, axis):
    return pltpu.roll(v, step % v.shape[axis], axis)


def fine_entries(width):
    found = []
    for way, distance in enumerate((width - 1, 1 - width, -width, width)):
        for slot in range(2):
            shift, other = divmod(slot + distance, 3)
            if other < 2:
                found.append((way, slot, shift, other))
    return found


def fine_kernel(
    width,
    start_ref,
    side_ref,
    top_ref,
    code_ref,
    cur_ref,
    reg_x_ref,
    reg_z_ref,
    base_ref,
    slab_x,
    slab_z,
    got_x,
    got_z,
    send_sem,
    recv_sem,
):
    here = lax.axis_index("wide")
    deep = lax.axis_index("deep")
    entries = fine_entries(width)
    edge, cells = cur_ref.shape[2:]
    lanes = slab_z.shape[4]
    shifts = sorted({e[2] % width for e in entries} | {-e[2] % width for e in entries})
    barrier = pltpu.get_barrier_semaphore()
    for shift in shifts:
        pl.semaphore_signal(
            barrier,
            inc=1,
            device_id=(lax.rem(here + shift, width), deep),
            device_id_type=pl.DeviceIdType.MESH,
        )
    cur_ref[...] = start_ref[...]
    base_ref[...] = start_ref[...]
    reg_x_ref[...] = jnp.zeros_like(reg_x_ref)
    reg_z_ref[...] = jnp.zeros_like(reg_z_ref)
    pl.semaphore_wait(barrier, len(shifts))

    def shift_y(v, k):
        step = k % edge
        ypos = lax.broadcasted_iota(jnp.int32, v.shape, 1) % edge
        return jnp.where(ypos < edge - step, roll(v, -step, 1), roll(v, edge - step, 1))

    def copies(stage):
        made = []
        counts = [0, 0]
        for number, (way, slot, shift, other) in enumerate(entries):
            kind = way // 2
            source = (slab_x, slab_z)[kind].at[other, 1 if way in (0, 2) else 0]
            target = (got_x, got_z)[kind].at[stage, counts[kind]]
            counts[kind] += 1
            made.append(
                pltpu.make_async_remote_copy(
                    src_ref=source,
                    dst_ref=target,
                    send_sem=send_sem.at[number],
                    recv_sem=recv_sem.at[stage, number],
                    device_id=(lax.rem(here + (-shift % width), width), deep),
                    device_id_type=pl.DeviceIdType.MESH,
                )
            )
        return made

    def one_stage(stage, carry):
        odd = stage % 2 == 1
        theta = 0.5 * ((stage + 1) // 2).astype(jnp.float32)
        for slot in range(2):
            for k in range(5):
                v = cur_ref[slot, k]
                slab_x[slot, 0, k] = v[:8]
                slab_x[slot, 1, k] = roll(v, 3, 0)[:8]
                slab_z[slot, 0, k] = v[:, :lanes]
                slab_z[slot, 1, k] = roll(v, 3 * edge, 1)[:, :lanes]
        sends = copies(stage)
        for copy in sends:
            copy.start()
        changes = []
        for slot in range(2):
            flux = shifted_flux(primitive([cur_ref[slot, k] for k in range(5)]), 2, shift_y)
            changes.append([f - shift_y(f, -1) for f in flux])
        for copy in sends:
            copy.wait_recv()

        def ghost(slot, way, k):
            code = code_ref[slot, way]
            kind, side = divmod(way, 2)
            rim = (side_ref, top_ref)[kind]
            value = (1.0 - theta) * rim[slot, 0, side, k] + theta * rim[slot, 1, side, k]
            same = [e for e in entries if e[0] // 2 == kind]
            for index, entry in enumerate(same):
                if entry[0] == way and entry[1] == slot:
                    value = jnp.where(code == 1, (got_x, got_z)[kind][stage, index, k], value)
            if (slot, way) == (1, 0):
                value = jnp.where(code == 2, slab_x[0, 1, k], value)
            if (slot, way) == (0, 1):
                value = jnp.where(code == 2, slab_x[1, 0, k], value)
            return value

        for slot in range(2):
            change = changes[slot]
            padded = []
            for k in range(5):
                v = cur_ref[slot, k]
                centre = roll(jnp.concatenate([v, v[:8]], axis=0), 3, 0)
                low = ghost(slot, 0, k)
                rim = jnp.concatenate([low, low, roll(ghost(slot, 1, k), 3, 0)], axis=0)
                row = lax.broadcasted_iota(jnp.int32, rim.shape, 0)
                outer = (row < 3) | ((row >= edge + 3) & (row < edge + 6))
                padded.append(jnp.where(outer, rim, centre))
            flux = shifted_flux(primitive(padded), 1, lambda v, k: roll(v, -k, 0))
            for k in range(5):
                reg_x_ref[slot, 0, k] += flux[k][:8]
                reg_x_ref[slot, 1, k] += flux[k][edge:]
                change[k] = change[k] + roll(flux[k] - roll(flux[k], 1, 0), -3, 0)[:edge]
            padded = []
            for k in range(5):
                v = cur_ref[slot, k]
                centre = roll(jnp.concatenate([v, v[:, :lanes]], axis=1), 3 * edge, 1)
                low = ghost(slot, 2, k)
                fill = [low] * (cells // lanes)
                rim = jnp.concatenate(fill + [roll(ghost(slot, 3, k), 3 * edge, 1)], axis=1)
                lane = lax.broadcasted_iota(jnp.int32, rim.shape, 1)
                outer = (lane < 3 * edge) | (
                    (lane >= cells + 3 * edge) & (lane < cells + 6 * edge)
                )
                padded.append(jnp.where(outer, rim, centre))
            flux = shifted_flux(primitive(padded), 3, lambda v, k: roll(v, -k * edge, 1))
            for k in range(5):
                reg_z_ref[slot, 0, k] += flux[k][:, :lanes]
                reg_z_ref[slot, 1, k] += flux[k][:, cells:]
                total = change[k] + roll(flux[k] - roll(flux[k], edge, 1), -3 * edge, 1)[:, :cells]
                old = cur_ref[slot, k]
                base = jnp.where(odd, base_ref[slot, k], old)
                base_ref[slot, k] = base
                new = old - (fine_step / fine_spacing) * total
                cur_ref[slot, k] = jnp.where(odd, 0.5 * (base + new), new)
        for copy in sends:
            copy.wait_send()
        return carry

    lax.fori_loop(0, 4, one_stage, 0)


def fine_steps(width, start, side, top, codes):
    edge, cells = start.shape[2:]
    lanes = top.shape[5]
    entries = fine_entries(width)
    n_x = sum(e[0] < 2 for e in entries)
    vmem = pl.BlockSpec(memory_space=pltpu.VMEM)
    shape_x, shape_z = (5, 8, cells), (5, edge, lanes)
    return pl.pallas_call(
        partial(fine_kernel, width),
        in_specs=[vmem, vmem, vmem, pl.BlockSpec(memory_space=pltpu.SMEM)],
        out_specs=[vmem] * 3,
        out_shape=[
            jax.ShapeDtypeStruct(s, jnp.float32)
            for s in (start.shape, (2, 2) + shape_x, (2, 2) + shape_z)
        ],
        scratch_shapes=[
            pltpu.VMEM(start.shape, jnp.float32),
            pltpu.VMEM((2, 2) + shape_x, jnp.float32),
            pltpu.VMEM((2, 2) + shape_z, jnp.float32),
            pltpu.VMEM((4, n_x) + shape_x, jnp.float32),
            pltpu.VMEM((4, len(entries) - n_x) + shape_z, jnp.float32),
            pltpu.SemaphoreType.DMA((len(entries),)),
            pltpu.SemaphoreType.DMA((4, len(entries))),
        ],
        compiler_params=pltpu.CompilerParams(collective_id=0, has_side_effects=True),
    )(start, side, top, codes)


def coarse_kernel(second, base_ref, cur_ref, ghost_ref, out_ref, fx_ref, fz_ref):
    block = cur_ref.shape[1]
    left, right = [], []
    whole = [
        jnp.concatenate([ghost_ref[k, :3], cur_ref[k], ghost_ref[k, 3:]], axis=0) for k in range(5)
    ]
    for v in primitive(whole):
        d = v[1:] - v[:-1]
        n = block + 2
        upper, lower = edge_values(v[2 : 2 + n], d[:n], d[1 : 1 + n], d[2 : 2 + n], d[3 : 3 + n])
        left.append(upper[:-1])
        right.append(lower[1:])
    flux = hllc(left, right, 1)
    for k in range(5):
        fx_ref[k, 0] = flux[k][0]
        fx_ref[k, 1] = flux[k][block]
        out_ref[k] = flux[k][1:] - flux[k][:-1]
    prims = primitive([cur_ref[k] for k in range(5)])
    flux = shifted_flux(prims, 2, lambda v, k: roll(v, -k, 1))
    for k in range(5):
        out_ref[k] += flux[k] - roll(flux[k], 1, 1)
    prims = primitive([cur_ref[k] for k in range(5)])
    flux = shifted_flux(prims, 3, lambda v, k: roll(v, -k, 2))
    for k in range(5):
        fz_ref[k] = flux[k]
        change = out_ref[k] + flux[k] - roll(flux[k], 1, 2)
        new = cur_ref[k] - coarse_step * change
        out_ref[k] = 0.5 * (base_ref[k] + new) if second else new


def coarse_stage(second, base, state, layers, below, above):
    depth = state.shape[3]
    lanes = -(-(depth + 6) // 128) * 128
    cur = jnp.concatenate([below, state, above, state[..., : lanes - depth - 6]], axis=3)
    wide = [(0, 0, 0)] * 3 + [(3, lanes - depth - 3, 0)]
    one = jnp.float32(1.0)
    ghost = lax.pad(layers, one, wide)
    base = lax.pad(base, one, wide)
    shapes = [cur.shape, (5, 2) + cur.shape[2:], cur.shape]
    out, fx, fz = pl.pallas_call(
        partial(coarse_kernel, second),
        out_shape=[jax.ShapeDtypeStruct(s, jnp.float32) for s in shapes],
        interpret=INTERPRET,
    )(base, cur, ghost)
    return out[..., 3 : 3 + depth], fx[..., 3 : 3 + depth], fz[..., 2 : 3 + depth]


def ring(count):
    up = [(i, (i + 1) % count) for i in range(count)]
    return up, [(j, i) for i, j in up]


def halo(shard, axis, dim, width):
    up, down = ring(lax.axis_size(axis))
    length = shard.shape[dim]
    before = lax.ppermute(lax.slice_in_dim(shard, length - width, length, axis=dim), axis, up)
    after = lax.ppermute(lax.slice_in_dim(shard, 0, width, axis=dim), axis, down)
    return before, after


def mark(flag):
    return flag[:, None, None, None]


def select(flags, values):
    which = jnp.sum(
        flags.astype(jnp.int32) * jnp.arange(flags.shape[1], dtype=jnp.int32)[None], axis=1
    )
    return values[which]


def exchange(values):
    return lax.all_to_all(values, "wide", split_axis=0, concat_axis=0, tiled=True)


def spread_matrices(block):
    edge = 2 * block
    fine = np.arange(edge)
    face = np.zeros((block, block, edge, edge), np.float32)
    face[fine[None] // 2, fine[:, None] // 2, fine[:, None], fine[None]] = 1.0
    face = face.reshape(block * block, edge * edge)
    lanes = -(-3 * edge // 128) * 128
    top = np.zeros((block, 4, 2, lanes), np.float32)
    for side, chosen in enumerate(([0, 1, 1], [2, 2, 3])):
        for layer, source in enumerate(chosen):
            top[fine // 2, source, side, layer * edge + fine] = 1.0
    return face, top.reshape(4 * block, 2 * lanes)


def local(
    coarse_density,
    coarse_velocity,
    coarse_pressure,
    fine_density,
    fine_velocity,
    fine_pressure,
    patch_count,
    region_start,
):
    width = lax.axis_size("wide")
    here = lax.axis_index("wide")
    block = coarse_density.shape[0]
    depth = coarse_density.shape[2]
    places = depth // block - 2
    slots = fine_density.shape[1]
    edge = 2 * block
    cells = edge * edge
    blocks_all = width * places
    counts = patch_count[0]
    ends = jnp.cumsum(counts)
    begins = ends - counts
    total = ends[-1]
    anchor = region_start[0]
    face_matrix, top_matrix = spread_matrices(block)

    def locate(target):
        offset = (target - anchor) % blocks_all
        part = offset % 3
        rank = 2 * (offset // 3) + part
        live = (part < 2) & (rank < total)
        return live, jnp.minimum(offset // 3, width - 1)

    dest = jnp.arange(width, dtype=jnp.int32)
    pair = jnp.arange(2, dtype=jnp.int32)

    density = fine_density[0]
    velocity = fine_velocity[0]
    pressure = fine_pressure[0]
    initial = jnp.moveaxis(
        conserved(jnp.stack([density, velocity[:, 0], velocity[:, 1], velocity[:, 2], pressure])),
        0,
        1,
    )
    wanted = jnp.clip(2 * dest[:, None] + pair[None] - begins[here], 0, slots - 1)
    moved = exchange(initial[wanted])
    my_rank = 2 * here + pair
    holder = jnp.minimum(
        jnp.sum((my_rank[:, None] >= ends[None]).astype(jnp.int32), axis=1), width - 1
    )

    coarse = conserved(
        jnp.stack(
            [
                coarse_density,
                coarse_velocity[0],
                coarse_velocity[1],
                coarse_velocity[2],
                coarse_pressure,
            ]
        )
    )
    old_xl, old_xh = halo(coarse, "wide", 1, 3)
    zl, zh = halo(coarse, "deep", 3, 3)
    middle, early_x, early_z = coarse_stage(
        False, coarse, coarse, jnp.concatenate([old_xl, old_xh], axis=1), zl, zh
    )
    xl, xh = halo(middle, "wide", 1, 3)
    zl, zh = halo(middle, "deep", 3, 3)
    updated, later_x, later_z = coarse_stage(
        True, coarse, middle, jnp.concatenate([xl, xh], axis=1), zl, zh
    )
    mean_x = 0.5 * (early_x + later_x)
    mean_z = 0.5 * (early_z + later_z)
    new_xl, new_xh = halo(updated, "wide", 1, 2)

    updated, moved = lax.optimization_barrier((updated, moved))
    start = jnp.stack([moved[holder[0], 0], moved[holder[1], 1]])
    height_ids = jnp.arange(places, dtype=jnp.int32)
    local_ident = height_ids * width + here
    live_here, device_here = locate(local_ident)
    to_device = live_here[None] & (device_here[None] == dest[:, None])
    bottom = block * (1 + jnp.sum(jnp.where(to_device, height_ids[None], 0), axis=1))
    cell_ids = jnp.arange(depth, dtype=jnp.int32)

    def one_hot(offsets, flags):
        found = cell_ids == (bottom[:, None] + np.array(offsets, np.int32))[..., None]
        return (found & flags[:, None, None]).astype(jnp.float32)

    inside = one_hot(range(block), jnp.any(to_device, axis=1))
    around = one_hot((-2, -1, block, block + 1), jnp.any(to_device, axis=1))
    sides = jnp.stack(
        [
            jnp.concatenate([low[:, -2:], high[:, :2]], axis=1)
            for low, high in ((old_xl, old_xh), (new_xl, new_xh))
        ]
    ).reshape(-1, depth)
    planes = jnp.stack([coarse, updated]).reshape(-1, depth)
    items = jnp.concatenate(
        [
            jnp.einsum("dzn,mn->dzm", inside, sides, precision=HIGHEST).reshape(width, -1),
            jnp.einsum("dln,mn->dlm", around, planes, precision=HIGHEST).reshape(width, -1),
        ],
        axis=1,
    )
    received = exchange(items.reshape(width, -1, 128))

    my_ident = (anchor + 3 * here + pair) % blocks_all
    my_column = my_ident % width
    my_height = my_ident // width
    rims = received[my_column].reshape(2, -1)
    side_rims = rims[:, : 40 * block * block].reshape(2, block, 2, 5, 4, block)
    top_rims = rims[:, 40 * block * block :].reshape(2, 4, 2, 5, block, block)
    face_rows = face_matrix.reshape(block, block, cells)
    spread = jnp.einsum("pztcly,yzn->ptcln", side_rims, face_rows, precision=HIGHEST)
    top_rows = top_matrix.reshape(block, 4, -1)
    top_spread = jnp.einsum("pltcxy,yln->ptcxn", top_rims, top_rows, precision=HIGHEST)
    filler = jnp.zeros(spread.shape[:3] + (5, cells), jnp.float32)
    side_ghosts = jnp.stack(
        [
            jnp.concatenate([spread[:, :, :, :2], spread[:, :, :, 1:2], filler], axis=3),
            jnp.concatenate([spread[:, :, :, 2:3], spread[:, :, :, 2:], filler], axis=3),
        ],
        axis=2,
    )
    top_ghosts = jnp.repeat(top_spread, 2, axis=3)
    lanes = top_ghosts.shape[4] // 2
    top_ghosts = jnp.stack([top_ghosts[..., :lanes], top_ghosts[..., lanes:]], axis=2)

    wrap_low = my_column == 0
    wrap_high = my_column == width - 1
    row_ident = my_height * width
    live_xl = locate(row_ident + (my_column + width - 1) % width)[0]
    live_xh = locate(row_ident + (my_column + 1) % width)[0]
    live_zl = locate(my_ident - width)[0] & (my_height > 0)
    live_zh = locate(my_ident + width)[0] & (my_height < places - 1)

    codes = jnp.stack(
        [
            jnp.where(live_xl, jnp.where(wrap_low, 1, 2), 0),
            jnp.where(live_xh, jnp.where(wrap_high, 1, 2), 0),
            jnp.where(live_zl, 1, 0),
            jnp.where(live_zh, 1, 0),
        ],
        axis=1,
    ).astype(jnp.int32)
    states, reg_x, reg_z = fine_steps(width, start, side_ghosts, top_ghosts, codes)

    face_mean = face_matrix.T * 0.25
    side_regs = jnp.dot(
        reg_x[:, :, :, 2], face_mean * (0.5 * fine_step), precision=HIGHEST
    )
    tops = reg_z[..., 2 * edge : 3 * edge].reshape(2, 2, 5, block, 2, edge).sum(axis=4)
    half = np.repeat(np.eye(block, dtype=np.float32), 2, axis=0) * (0.25 * 0.5 * fine_step)
    top_regs = jnp.dot(tops, half, precision=HIGHEST)
    pooled = states.reshape(2, 5, block, 2, cells).sum(axis=3)
    averaged = jnp.dot(pooled, face_mean * 0.5, precision=HIGHEST)
    averaged = averaged.reshape(2, 5, block, block, block)
    side_regs = side_regs.reshape(2, 2, 5, block, block)
    package = jnp.concatenate(
        [
            jnp.moveaxis(averaged, 4, 1).reshape(2, -1),
            top_regs.reshape(2, -1),
            jnp.moveaxis(side_regs, 4, 2).reshape(2, -1),
        ],
        axis=1,
    ).reshape(2, -1, 128)
    to_brick = my_column[None] == dest[:, None]
    brought = exchange(select(to_brick, package))
    brought = brought.reshape(width, -1)
    face = 5 * block * block
    main = brought[:, : (block + 2) * face].reshape(width, block + 2, face)
    side_part = brought[:, (block + 2) * face :].reshape(width, 2, block, 5 * block)
    edge_xl = live_here & ~locate(height_ids * width + (here + width - 1) % width)[0]
    edge_xh = live_here & ~locate(height_ids * width + (here + 1) % width)[0]
    edge_zl = live_here & ~(locate(local_ident - width)[0] & (height_ids > 0))
    edge_zh = live_here & ~(locate(local_ident + width)[0] & (height_ids < places - 1))

    def with_edge(flags):
        return jnp.any(to_device & flags[None], axis=1)

    def at_cells(flags, first, count):
        padded = jnp.pad(jnp.repeat(flags, block), (block, block))
        phase = cell_ids % block
        return padded & (phase >= first) & (phase < first + count)

    def side_terms(side, flags):
        chosen = inside * with_edge(flags)[:, None, None].astype(jnp.float32)
        term = jnp.einsum("dzm,dzn->mn", side_part[:, side], chosen, precision=HIGHEST)
        coarse_part = jnp.where(at_cells(flags, 0, block), coarse_step * mean_x[:, side], 0.0)
        return coarse_part - term.reshape(coarse_part.shape)

    up, down = ring(width)
    to_first = lax.ppermute(-side_terms(1, edge_xh), "wide", up)
    to_last = lax.ppermute(side_terms(0, edge_xl), "wide", down)
    to_first, to_last, states = lax.optimization_barrier((to_first, to_last, states))
    back = exchange(jnp.broadcast_to(states[None], (width,) + states.shape))
    slot_ids = jnp.arange(slots, dtype=jnp.int32)
    my_alive = slot_ids < counts[here]
    serial = jnp.clip(begins[here] + slot_ids, 0, 2 * width - 1)
    final_fine = back.reshape((2 * width,) + back.shape[2:])[serial]
    fine_out = jnp.where(mark(my_alive), final_fine, initial)[None]

    rows = jnp.concatenate(
        [
            inside,
            -one_hot((-1,), with_edge(edge_zl)),
            one_hot((block,), with_edge(edge_zh)),
        ],
        axis=1,
    )
    placed = jnp.einsum("dkm,dkn->mn", main, rows, precision=HIGHEST).reshape(updated.shape)
    below_low = jnp.roll(at_cells(edge_zl, 0, 1), -1)
    above_high = jnp.roll(at_cells(edge_zh, block - 1, 1), 1)
    result = updated + jnp.where(below_low, coarse_step * mean_z[..., 1:], 0.0)
    result = result - jnp.where(above_high, coarse_step * mean_z[..., :-1], 0.0)
    layer = jnp.arange(block)[None, :, None, None]
    result = result + jnp.where(layer == 0, to_first[:, None], 0.0)
    result = result + jnp.where(layer == block - 1, to_last[:, None], 0.0)
    return jnp.where(at_cells(live_here, 0, block), 0.0, result) + placed, fine_out


def solution(mesh):
    return jax.shard_map(
        local,
        mesh=mesh,
        in_specs=(
            P("wide", None, "deep"),
            P(None, "wide", None, "deep"),
            P("wide", None, "deep"),
            P("deep", "wide", None, None),
            P("deep", "wide", None, None, None),
            P("deep", "wide", None, None),
            P("deep", None),
            P("deep"),
        ),
        out_specs=(P(None, "wide", None, "deep"), P("deep", "wide", None, None, None)),
        check_vma=False,
    )
```
